768 devices in a mesh: lat: 24 (over z, core), lon: 32 (over x, y).
Axes of the slice: x: 4, y: 8, z: 12, core: 2. Of those that a mesh axis runs over, the one named last changes fastest.
Arguments:
- ensemble: float32 [768, 4096, 128], P('lat', 'lon'), may hold values from -6 to 6
- observed: float32 [2, 24, 32, 8], P(None, 'lat', 'lon'), may hold values from -8 to 8
- precision: float32 [2, 24, 32, 8], P(None, 'lat', 'lon'), may hold values from 0.05 to 0.5
- interp_weight: float32 [2, 24, 32, 4, 8], P(None, 'lat', 'lon'), may hold values from 0.1 to 1
- stencil: int32 [2, 24, 32, 4, 8], P(None, 'lat', 'lon'), may hold values from 0 to 4419, as said below
- owned: int32 [2, 24, 32, 8], P(None, 'lat', 'lon'), may hold values from 0 to 1, as said below
- pattern: int32 [2, 24, 32, 5, 32], P(None, 'lat', 'lon'), may hold values 0 or 1
Outputs:
- analysis: float32 [768, 4096, 128], P('lat', 'lon')
The draws below stay inside these ranges and needn't reach their ends.
Inputs may be any that keep to these rules, and one draw needn't show every extreme that they name: `stencil`: each index names one of the four corners of a 2 x 2 square of cells of the rim-extended tile, in the order (0,0), (0,1), (1,0), (1,1). In each batch and tile the owned slots come first and there is at least one; some tile owns all 8 slots in every batch.
All inputs are finite; a program needn't handle non-finite values. No bound on the sum of `pattern` on one device may be relied on, other than what follows from the above.
Results may differ from the reference program's by a relative error of at most 0.0026.
Values may be sent and summed in bfloat16 or wider, within the bound.
A program may use at most 32 MiB of HBM per device.

```python
import math
import jax
import jax.numpy as jnp
from jax import lax

MEMBERS = 128
CELLS_LAT = 32
CELLS_LON = 128
OBS_DEV = 8
BATCHES = 2
REACH = 2
WIN = 5
TILES_LAT = 24
TILES_LON = 32
GRID_LAT = 768
GRID_LON = 4096


def draw_stencil(key, part):
    first_key, second_key = jax.random.split(jax.random.fold_in(key, 11))
    base_row = jax.random.randint(first_key, (BATCHES, TILES_LAT, TILES_LON, 1, OBS_DEV), 0, CELLS_LAT + 1)
    base_col = jax.random.randint(second_key, (BATCHES, TILES_LAT, TILES_LON, 1, OBS_DEV), 0, CELLS_LON + 1)
    corner = jnp.array([0, 1, CELLS_LON + 2, CELLS_LON + 3], jnp.int32).reshape(1, 1, 1, 4, 1)
    return (base_row * (CELLS_LON + 2) + base_col + corner).astype(jnp.int32)


def draw_owned(key, part):
    counts = jax.random.randint(jax.random.fold_in(key, 23), (BATCHES, TILES_LAT, TILES_LON, 1), 1, OBS_DEV + 1)
    counts = counts.at[:, 0, 0, :].set(OBS_DEV)
    slots = jnp.arange(OBS_DEV, dtype=jnp.int32).reshape(1, 1, 1, -1)
    return (slots < counts).astype(jnp.int32)


def with_ends(values, own_key, smallest, largest):
    extent = values.shape
    place = [jax.random.randint(jax.random.fold_in(own_key, axis), (), 0, extent[axis]) for axis in range(len(extent))]
    values = values.at[tuple(place)].set(smallest)
    longest = extent.index(max(extent))
    place[longest] = (place[longest] + 1) % extent[longest]
    return values.at[tuple(place)].set(largest)


def levels(own_key, dims, pieces, least, top_value):
    level = 1.0
    for position, parts in pieces:
        steps = jax.random.uniform(jax.random.fold_in(jax.random.fold_in(own_key, 6), position), (parts,), jnp.float32, least / len(pieces), top_value / len(pieces))
        level = level * jnp.repeat(jnp.exp(steps), dims[position] // parts).reshape((-1,) + (1,) * (len(dims) - 1 - position))
    return level


def gaussian(rng, shape, deviation, reach, shards=(), held_as=jnp.bfloat16):
    loudness = levels(rng, shape, shards, -0.22, 0.18) if shards else 1.0
    values = jax.random.normal(rng, shape, jnp.float32) * deviation * loudness
    return jnp.minimum(jnp.maximum(values, -reach), reach).astype(held_as)


def setup_inputs(seed: int = 0) -> dict:
    key_list = jax.random.split(jax.random.key(seed), 8)
    return {
        "ensemble": gaussian(key_list[0], (GRID_LAT, GRID_LON, MEMBERS), 1.0, 6.0, ((0, 24), (1, 32)), jnp.float32),
        "observed": gaussian(key_list[1], (BATCHES, TILES_LAT, TILES_LON, OBS_DEV), 1.5, 8.0, ((1, 24), (2, 32)), jnp.float32),
        "precision": jnp.clip(jnp.exp(math.log(0.5) - 2.3025851 * jax.random.uniform(key_list[2], (BATCHES, TILES_LAT, TILES_LON, OBS_DEV), jnp.float32) ** levels(key_list[2], (BATCHES, TILES_LAT, TILES_LON, OBS_DEV), ((1, 24), (2, 32)), -0.2, 0.2)), 0.05, 0.5),
        "interp_weight": jnp.clip(0.1 + 0.9 * jax.random.uniform(key_list[3], (BATCHES, TILES_LAT, TILES_LON, 4, OBS_DEV), jnp.float32) ** levels(key_list[3], (BATCHES, TILES_LAT, TILES_LON, 4, OBS_DEV), ((1, 24), (2, 32)), -0.2, 0.2), 0.1, 1.0),
        "stencil": draw_stencil(jax.random.fold_in(key_list[7], 71), 0),
        "owned": draw_owned(jax.random.fold_in(key_list[7], 71), 0),
        "pattern": with_ends((jax.random.randint(key_list[6], (BATCHES, TILES_LAT, TILES_LON, WIN, TILES_LON), 0, 2) < 1).astype(jnp.int32), jax.random.fold_in(key_list[6], 1), 0, 1),
    }


def square_root(gram, proj):
    members = gram.shape[-1]
    eye = jnp.eye(members, dtype=jnp.float32)
    system = gram + (members - 1.0) * eye
    factor = jnp.linalg.cholesky(system)
    lower_sol = jax.scipy.linalg.solve_triangular(factor, proj[..., None], lower=True)
    weights = jax.scipy.linalg.solve_triangular(factor, lower_sol, lower=True, trans=1)
    inverse = jax.scipy.linalg.solve_triangular(factor, jnp.broadcast_to(eye, system.shape), lower=True)
    return jnp.sqrt(members - 1.0) * jnp.swapaxes(inverse, -1, -2) + weights

def reference(ensemble, observed, precision, interp_weight, stencil, owned, pattern):
    analysis = ensemble
    tile_row = (jnp.arange(TILES_LAT, dtype=jnp.int32) * CELLS_LAT).reshape(-1, 1, 1, 1)
    tile_col = (jnp.arange(TILES_LON, dtype=jnp.int32) * CELLS_LON).reshape(1, -1, 1, 1)
    for batch_no in range(BATCHES):
        wrapped = jnp.concatenate([analysis[:, -1:], analysis, analysis[:, :1]], axis=1)
        padded = jnp.pad(wrapped, ((1, 1), (0, 0), (0, 0)))
        cells = stencil[batch_no]
        in_row = cells // (CELLS_LON + 2)
        in_col = cells % (CELLS_LON + 2)
        values = padded[tile_row + in_row, tile_col + in_col]
        prior = lax.optimization_barrier(jnp.sum(interp_weight[batch_no][..., None] * values, axis=2))
        mean_prior = lax.optimization_barrier(jnp.mean(prior, axis=-1))
        root = jnp.sqrt(precision[batch_no]) * owned[batch_no].astype(jnp.float32)
        scaled = (root[..., None] * (prior - mean_prior[..., None])).astype(jnp.bfloat16)
        innov = (root * (observed[batch_no] - mean_prior)).astype(jnp.bfloat16)
        scaled_f = scaled.astype(jnp.float32)
        innov_f = innov.astype(jnp.float32)
        blocks = jnp.einsum('acom,acon->acmn', scaled_f, scaled_f, precision=lax.Precision.HIGHEST)
        vectors = jnp.einsum('acom,aco->acm', scaled_f, innov_f, precision=lax.Precision.HIGHEST)
        pad_blocks = jnp.pad(blocks, ((REACH, REACH), (0, 0), (0, 0), (0, 0)))
        pad_vectors = jnp.pad(vectors, ((REACH, REACH), (0, 0), (0, 0)))
        marks = pattern[batch_no].astype(jnp.float32)
        gram = jnp.zeros((TILES_LAT, TILES_LON, MEMBERS, MEMBERS), jnp.float32)
        proj = jnp.zeros((TILES_LAT, TILES_LON, MEMBERS), jnp.float32)
        for offset in range(WIN):
            gram = gram + jnp.einsum('ace,aemn->acmn', marks[:, :, offset], pad_blocks[offset:offset + TILES_LAT], precision=lax.Precision.HIGHEST)
            proj = proj + jnp.einsum('ace,aem->acm', marks[:, :, offset], pad_vectors[offset:offset + TILES_LAT], precision=lax.Precision.HIGHEST)
        transform = square_root(gram, proj)
        tiles = analysis.reshape(TILES_LAT, CELLS_LAT, TILES_LON, CELLS_LON, MEMBERS)
        center = lax.optimization_barrier(jnp.mean(tiles, axis=-1, keepdims=True))
        moved = jnp.einsum('axcym,acmn->axcyn', tiles - center, transform, precision=lax.Precision.HIGHEST)
        analysis = (center + moved).reshape(GRID_LAT, GRID_LON, MEMBERS)
    return analysis
```

```python
import functools
import math
import jax
import jax.numpy as jnp
from jax import lax
from jax.experimental import pallas as pl
from jax.experimental.pallas import tpu as pltpu
from jax.sharding import PartitionSpec as P

MESH = pl.DeviceIdType.MESH
F32 = jnp.float32
BF16 = jnp.bfloat16
ROWS, COLS, N = 32, 128, 128
SLOTS = 8
LATS, LONS = 24, 32
YS, XS = 8, 4
TOP, BOTTOM, LEFT, RIGHT, BLANK = 0, COLS + 2, 2 * (COLS + 2), 2 * (COLS + 2) + ROWS, 2 * (COLS + 2) + 2 * ROWS
RIM = BLANK + 1
NB = N // 8
NEAR = (-2, -1, 1, 2)
VMEM_BYTES = 48 * 2**20


def split3(x):
    high = x.astype(BF16).astype(F32)
    rest = x - high
    mid = rest.astype(BF16).astype(F32)
    return high, mid, rest - mid


def outer8(r, g):
    rh, rm, rl = split3(r)
    gh, gm, gl = split3(g)
    lhs = jnp.concatenate([rh, rh, rm, rh, rl, rm], axis=0).astype(BF16)
    rhs = jnp.concatenate([gh, gm, gh, gl, gh, gm], axis=0).astype(BF16)
    return lax.dot_general(lhs, rhs, (((0,), (0,)), ((), ())), preferred_element_type=F32)


def spread_row(x, k):
    return jnp.broadcast_to(x[k : k + 1, :], (8, N))


def spread_col(x, c):
    return jnp.broadcast_to(x[:, c : c + 1], (8, N))


def transform_t(gram, proj):
    lane = lax.broadcasted_iota(jnp.int32, (8, N), 1)
    sub = lax.broadcasted_iota(jnp.int32, (8, N), 0)
    prow = jnp.broadcast_to(proj, (8, N))
    w = [gram[8 * i : 8 * i + 8, :] + jnp.where(lane == sub + 8 * i, N - 1.0, 0.0) for i in range(NB)]
    inverse, sums = [], []
    acc = jnp.zeros((8, N), F32)
    for j in range(NB):
        c0 = 8 * j
        wj = w[j]
        cols = [spread_col(wj, c0 + k) for k in range(8)]
        here = (lane >= c0) & (lane < c0 + 8)
        f = jnp.where(here, jnp.where(lane == sub + c0, 1.0, 0.0), wj)
        lower, diag = f, cols[0]
        for k in range(8):
            inv = 1.0 / spread_row(cols[k], k)
            if k:
                lower = jnp.where(sub == k, f, lower)
                diag = jnp.where(sub == k, cols[k], diag)
            m = jnp.where(sub == k, 0.0, cols[k] * inv)
            for t in range(k + 1, 8):
                cols[t] = cols[t] - m * spread_row(cols[t], k)
            f = f - m * spread_row(f, k)
        g = f * (1.0 / diag)
        lj = jnp.where(lane <= c0 + 7, lower * lax.rsqrt(diag), 0.0)
        inverse.append(lj)
        sums.append(jnp.sum(lj, axis=1, keepdims=True))
        acc = acc + lj * jnp.sum(lj * prow, axis=1, keepdims=True)
        if j < NB - 1:
            nxt = w[j + 1]
            upd = jnp.where(here, 0.0, nxt)
            for k in range(8):
                upd = upd - spread_col(nxt, c0 + k) * spread_row(g, k)
            if j < NB - 2:
                p = outer8(wj, g)
                for i in range(j + 2, NB):
                    w[i] = jnp.where(here, 0.0, w[i]) - p[8 * i : 8 * i + 8, :]
            w[j + 1] = upd
    weights = jnp.sum(acc, axis=0, keepdims=True)
    total = jnp.sum(weights, axis=1, keepdims=True)
    root = math.sqrt(N - 1.0)
    out = []
    for i in range(NB):
        fix = (1.0 - (root * sums[i] + total)) * (1.0 / N)
        out.append(root * inverse[i] + weights + fix)
    return jnp.concatenate(out, axis=0)


def times(x, tt):
    return lax.dot_general(
        x, tt, (((1,), (1,)), ((), ())), precision=lax.Precision.HIGHEST, preferred_element_type=F32
    )


def position():
    lat, lon = lax.axis_index("lat"), lax.axis_index("lon")
    return lat, lon, lon // YS, lax.rem(lon, YS)


def inside(lat, step):
    return (lat + step >= 0) & (lat + step < LATS)


def enter(lat, lon, x, y):
    barrier = pltpu.get_barrier_semaphore()

    def greet(a, c):
        pl.semaphore_signal(barrier, inc=1, device_id=(a, c), device_id_type=MESH)

    east, west = lax.rem(lon + 1, LONS), lax.rem(lon + LONS - 1, LONS)
    greet(lat, east)
    greet(lat, west)
    for t in range(1, YS):
        greet(lat, x * YS + lax.rem(y + t, YS))
    for t in range(1, XS):
        greet(lat, lax.rem(x + t, XS) * YS + y)
    for step in NEAR:

        @pl.when(inside(lat, step))
        def _():
            greet(lat + step, lon)
            if abs(step) == 1:
                greet(lat + step, east)
                greet(lat + step, west)

    count = YS - 1 + XS - 1 + 2
    for step in NEAR:
        count = count + jnp.where(inside(lat, step), 3 if abs(step) == 1 else 1, 0)
    pl.semaphore_wait(barrier, count)


def masks(batch, pattern_ref, mark, markv):
    @pl.loop(0, 5 * LONS)
    def _(i):
        value = pattern_ref[batch, i // LONS, lax.rem(i, LONS)].astype(F32)
        mark[i] = jnp.full((SLOTS, N), value, F32).astype(BF16)
        markv[i] = jnp.full((1, N), value, F32)


def blank_rows(lat, seen, seenv):
    for step in NEAR:

        @pl.when(jnp.logical_not(inside(lat, step)))
        def _():
            d = step + 2
            seen[pl.ds(d * LONS, LONS)] = jnp.zeros((LONS, SLOTS, N), BF16)
            seenv[pl.ds(d * LONS, LONS)] = jnp.zeros((LONS, 1, N), F32)


def observe(batch, prior, observed_ref, precision_ref, owned_ref):
    sub = lax.broadcasted_iota(jnp.int32, (SLOTS, N), 0)
    obs = jnp.zeros((SLOTS, N), F32)
    prec = jnp.zeros((SLOTS, N), F32)
    own = jnp.zeros((SLOTS, N), F32)
    for o in range(SLOTS):
        obs = jnp.where(sub == o, observed_ref[batch, o], obs)
        prec = jnp.where(sub == o, precision_ref[batch, o], prec)
        own = jnp.where(sub == o, owned_ref[batch, o].astype(F32), own)
    root = jnp.sqrt(prec) * own
    mean = jnp.sum(prior, axis=1, keepdims=True) * (1.0 / N)
    scaled = (root * (prior - mean)).astype(BF16)
    innov = (root * (obs - mean)).astype(BF16)
    vector = jnp.sum(scaled.astype(F32) * innov.astype(F32), axis=0, keepdims=True)
    return scaled, vector


def spread_out(pos, seen, seenv, sems, mark, markv):
    lat, lon, x, y = pos
    mine = 2 * LONS

    def copy(ref, start, size, to, device, sem, slot):
        return pltpu.make_async_remote_copy(
            src_ref=ref.at[pl.ds(start, size)],
            dst_ref=ref.at[pl.ds(to, size)],
            send_sem=sem.at[0, slot],
            recv_sem=sem.at[1, slot],
            device_id=device,
            device_id_type=MESH,
        )

    def both(start, size, to, device, slot):
        return (
            copy(seen, start, size, to, device, sems[0], slot),
            copy(seenv, start, size, to, device, sems[1], slot),
        )

    stage_y = []
    for t in range(1, YS):
        device = (lat, x * YS + lax.rem(y + t, YS))
        stage_y += both(mine + lon, 1, mine + lon, device, t - 1)
    for c in stage_y:
        c.start()
    for c in stage_y:
        c.wait()
    stage_x = []
    for t in range(1, XS):
        device = (lat, lax.rem(x + t, XS) * YS + y)
        stage_x += both(mine + x * YS, YS, mine + x * YS, device, YS - 1 + t - 1)
    for c in stage_x:
        c.start()
    for c in stage_x:
        c.wait()

    def lat_copies(i, step):
        return both(mine, LONS, (2 - step) * LONS, (lat + step, lon), YS + XS - 2 + i)

    for i, step in enumerate(NEAR):

        @pl.when(inside(lat, step))
        def _():
            for c in lat_copies(i, step):
                c.start()

    def term(d):
        rows = seen[pl.ds(d * LONS, LONS)]
        marked = rows * mark[pl.ds(d * LONS, LONS)]
        gram = lax.dot_general(
            marked.reshape(LONS * SLOTS, N),
            rows.reshape(LONS * SLOTS, N),
            (((0,), (0,)), ((), ())),
            preferred_element_type=F32,
        )
        return gram, jnp.sum(seenv[pl.ds(d * LONS, LONS)] * markv[pl.ds(d * LONS, LONS)], axis=0)

    gram, proj = term(2)
    for i, step in enumerate(NEAR):

        @pl.when(inside(lat, step))
        def _():
            for c in lat_copies(i, step):
                c.wait_send()

        @pl.when(inside(lat, -step))
        def _():
            for c in lat_copies(i, step):
                c.wait_recv()

        g, v = term(2 - step)
        gram, proj = gram + g, proj + v
    return gram, proj


def corner(stencil_ref, batch, o):
    s = stencil_ref[batch, 0, o]
    r = s // (COLS + 2)
    return r, s - r * (COLS + 2)


def first_kernel(
    ens, observed, precision, weight, stencil, owned, pattern,
    gram_ref, proj_ref, raw_ref,
    tile, prior, seen, seenv, mark, markv, local_sem, halo_sem, sem_s, sem_v,
):
    pos = position()
    lat, lon, x, y = pos
    east, west = lax.rem(lon + 1, LONS), lax.rem(lon + LONS - 1, LONS)
    inner = pltpu.make_async_copy(ens, tile.at[pl.ds(1, ROWS), pl.ds(1, COLS)], local_sem)
    inner.start()
    for step, r in ((-1, 0), (1, ROWS + 1)):

        @pl.when(jnp.logical_not(inside(lat, step)))
        def _():
            tile[r] = jnp.zeros((COLS + 2, 1, N), F32)

    blank_rows(lat, seen, seenv)
    enter(lat, lon, x, y)

    def halo(src, dst, device, slot):
        return pltpu.make_async_remote_copy(
            src_ref=src, dst_ref=dst, send_sem=halo_sem.at[0, slot], recv_sem=halo_sem.at[1, slot],
            device_id=device, device_id_type=MESH,
        )

    sides = [
        halo(ens.at[:, COLS - 1], tile.at[pl.ds(1, ROWS), 0], (lat, east), 0),
        halo(ens.at[:, 0], tile.at[pl.ds(1, ROWS), COLS + 1], (lat, west), 1),
    ]

    def ends(step):
        r, to, slot = (ROWS - 1, 0, 2) if step == 1 else (0, ROWS + 1, 5)
        return [
            halo(ens.at[r], tile.at[to, pl.ds(1, COLS)], (lat + step, lon), slot),
            halo(ens.at[r, COLS - 1], tile.at[to, 0], (lat + step, east), slot + 1),
            halo(ens.at[r, 0], tile.at[to, COLS + 1], (lat + step, west), slot + 2),
        ]

    for step in (1, -1):

        @pl.when(inside(lat, step))
        def _():
            for c in ends(step):
                c.start()

    for c in sides:
        c.start()
    masks(0, pattern, mark, markv)
    inner.wait()
    for c in sides:
        c.wait()
    for step in (1, -1):

        @pl.when(inside(lat, step))
        def _():
            for c in ends(step):
                c.wait_send()

        @pl.when(inside(lat, -step))
        def _():
            for c in ends(step):
                c.wait_recv()

    for o in range(SLOTS):
        r, c = corner(stencil, 0, o)
        total = jnp.zeros((1, N), F32)
        for k in range(4):
            total = total + weight[0, k, o] * tile[r + k // 2, c + k % 2]
        prior[pl.ds(o, 1), :] = total
    for o in range(SLOTS):
        r, c = corner(stencil, 1, o)
        total = jnp.zeros((1, N), F32)
        for k in range(4):
            rk, ck = r + k // 2, c + k % 2
            own = (rk >= 1) & (rk <= ROWS) & (ck >= 1) & (ck <= COLS)
            total = total + jnp.where(own, weight[1, k, o], 0.0) * tile[rk, ck]
        raw_ref[pl.ds(o, 1), :] = total
    scaled, vector = observe(0, prior[...], observed, precision, owned)
    seen[2 * LONS + lon] = scaled
    seenv[2 * LONS + lon] = vector
    gram_ref[...], proj_ref[...] = spread_out(pos, seen, seenv, (sem_s, sem_v), mark, markv)


def second_kernel(
    rows_ref, sides_ref, held, observed, precision, weight, stencil, owned, pattern,
    gram_ref, proj_ref,
    rim, prior, seen, seenv, mark, markv, halo_sem, sem_s, sem_v,
):
    pos = position()
    lat, lon, x, y = pos
    east, west = lax.rem(lon + 1, LONS), lax.rem(lon + LONS - 1, LONS)
    rim[BLANK] = jnp.zeros((1, N), F32)
    for step, r in ((-1, TOP), (1, BOTTOM)):

        @pl.when(jnp.logical_not(inside(lat, step)))
        def _():
            rim[pl.ds(r, COLS + 2)] = jnp.zeros((COLS + 2, 1, N), F32)

    blank_rows(lat, seen, seenv)
    enter(lat, lon, x, y)

    def halo(src, dst, device, slot):
        return pltpu.make_async_remote_copy(
            src_ref=src, dst_ref=dst, send_sem=halo_sem.at[0, slot], recv_sem=halo_sem.at[1, slot],
            device_id=device, device_id_type=MESH,
        )

    sides = [
        halo(sides_ref.at[1], rim.at[pl.ds(LEFT, ROWS)], (lat, east), 0),
        halo(sides_ref.at[0], rim.at[pl.ds(RIGHT, ROWS)], (lat, west), 1),
    ]

    def ends(step):
        r, to, slot = (1, TOP, 2) if step == 1 else (0, BOTTOM, 5)
        return [
            halo(rows_ref.at[r], rim.at[pl.ds(to + 1, COLS)], (lat + step, lon), slot),
            halo(rows_ref.at[r, pl.ds(COLS - 1, 1)], rim.at[pl.ds(to, 1)], (lat + step, east), slot + 1),
            halo(rows_ref.at[r, pl.ds(0, 1)], rim.at[pl.ds(to + COLS + 1, 1)], (lat + step, west), slot + 2),
        ]

    for step in (1, -1):

        @pl.when(inside(lat, step))
        def _():
            for c in ends(step):
                c.start()

    for c in sides:
        c.start()
    masks(1, pattern, mark, markv)
    for c in sides:
        c.wait()
    for step in (1, -1):

        @pl.when(inside(lat, step))
        def _():
            for c in ends(step):
                c.wait_send()

        @pl.when(inside(lat, -step))
        def _():
            for c in ends(step):
                c.wait_recv()

    for o in range(SLOTS):
        r, c = corner(stencil, 1, o)
        total = held[pl.ds(o, 1), :]
        for k in range(4):
            rk, ck = r + k // 2, c + k % 2
            where = jnp.where(ck == 0, LEFT - 1 + rk, jnp.where(ck == COLS + 1, RIGHT - 1 + rk, BLANK))
            where = jnp.where(rk == 0, TOP + ck, jnp.where(rk == ROWS + 1, BOTTOM + ck, where))
            total = total + weight[1, k, o] * rim[where]
        prior[pl.ds(o, 1), :] = total
    scaled, vector = observe(1, prior[...], observed, precision, owned)
    seen[2 * LONS + lon] = scaled
    seenv[2 * LONS + lon] = vector
    gram_ref[...], proj_ref[...] = spread_out(pos, seen, seenv, (sem_s, sem_v), mark, markv)


def between_kernel(gram, proj, raw, ens, ens_cells, tt_ref, held_ref, rows_ref, sides_ref, edge, strip, sems):
    copies = [
        pltpu.make_async_copy(ens.at[0], edge.at[0], sems.at[0]),
        pltpu.make_async_copy(ens.at[ROWS - 1], edge.at[1], sems.at[1]),
        pltpu.make_async_copy(ens_cells.at[:, 0], strip.at[0], sems.at[2]),
        pltpu.make_async_copy(ens_cells.at[:, COLS - 1], strip.at[1], sems.at[3]),
    ]
    for c in copies:
        c.start()
    tt = transform_t(gram[...], proj[...])
    tt_ref[...] = tt
    for c in copies:
        c.wait()
    held_ref[...] = times(raw[...], tt)
    for i in range(2):
        rows_ref[i] = times(edge[i], tt).reshape(COLS, 1, N)
        sides_ref[i] = times(strip[i].reshape(ROWS, N), tt).reshape(ROWS, 1, N)


CHUNK = 512


def last_kernel(gram, proj, tt_ref, ens, out, cells, moved, in_sem, out_sem):
    chunks = ROWS * COLS // CHUNK
    loads = [
        pltpu.make_async_copy(ens.at[pl.ds(i * CHUNK, CHUNK)], cells.at[pl.ds(i * CHUNK, CHUNK)], in_sem.at[i])
        for i in range(chunks)
    ]
    for c in loads:
        c.start()
    tt = transform_t(gram[...], proj[...])
    both = jnp.dot(tt, tt_ref[...], precision=lax.Precision.HIGHEST, preferred_element_type=F32)
    high = both.astype(BF16)
    low = (both - high.astype(F32)).astype(BF16)
    right = jnp.concatenate(
        [jnp.concatenate([high, high], axis=1), jnp.concatenate([low, jnp.zeros_like(low)], axis=1)], axis=0
    )
    stores = []
    for i in range(chunks):
        rows = pl.ds(i * CHUNK, CHUNK)
        loads[i].wait()
        xs = cells[rows, :]
        xh = xs.astype(BF16)
        xl = (xs - xh.astype(F32)).astype(BF16)
        res = lax.dot_general(
            jnp.concatenate([xh, xl], axis=1), right, (((1,), (1,)), ((), ())), preferred_element_type=F32
        )
        moved[rows, :] = res[:, :N] + res[:, N:]
        c = pltpu.make_async_copy(moved.at[rows], out.at[rows], out_sem.at[i])
        c.start()
        stores.append(c)
    for c in stores:
        c.wait()


def shape(*dims):
    return jax.ShapeDtypeStruct(dims, F32)


VM = pl.BlockSpec(memory_space=pltpu.VMEM)
SM = pl.BlockSpec(memory_space=pltpu.SMEM)
ANY = pl.BlockSpec(memory_space=pl.ANY)


def exchange_scratch():
    return [
        pltpu.VMEM((SLOTS, N), F32),
        pltpu.VMEM((5 * LONS, SLOTS, N), BF16),
        pltpu.VMEM((5 * LONS, 1, N), F32),
        pltpu.VMEM((5 * LONS, SLOTS, N), BF16),
        pltpu.VMEM((5 * LONS, 1, N), F32),
    ]


def exchange_sems():
    count = YS - 1 + XS - 1 + len(NEAR)
    return [
        pltpu.SemaphoreType.DMA((2, 8)),
        pltpu.SemaphoreType.DMA((2, count)),
        pltpu.SemaphoreType.DMA((2, count)),
    ]


def local(ensemble, observed, precision, interp_weight, stencil, owned, pattern):
    cells = ensemble.reshape(ROWS, COLS, 1, N)
    small = (
        observed.reshape(2, SLOTS),
        precision.reshape(2, SLOTS),
        interp_weight.reshape(2, 4, SLOTS),
        stencil.reshape(2, 4, SLOTS),
        owned.reshape(2, SLOTS),
        pattern.reshape(2, 5, LONS),
    )
    gram, proj, raw = pl.pallas_call(
        first_kernel,
        out_shape=(shape(N, N), shape(1, N), shape(SLOTS, N)),
        in_specs=[ANY] + [SM] * 6,
        out_specs=(VM, VM, VM),
        scratch_shapes=[pltpu.VMEM((ROWS + 2, COLS + 2, 1, N), F32)]
        + exchange_scratch()
        + [pltpu.SemaphoreType.DMA]
        + exchange_sems(),
        compiler_params=pltpu.CompilerParams(collective_id=0, has_side_effects=True, vmem_limit_bytes=VMEM_BYTES),
        name="first",
    )(cells, *small)
    tt, held, rows, sides = pl.pallas_call(
        between_kernel,
        out_shape=(shape(N, N), shape(SLOTS, N), shape(2, COLS, 1, N), shape(2, ROWS, 1, N)),
        in_specs=[VM, VM, VM, ANY, ANY],
        out_specs=(VM, VM, VM, VM),
        scratch_shapes=[
            pltpu.VMEM((2, COLS, N), F32),
            pltpu.VMEM((2, ROWS, 1, N), F32),
            pltpu.SemaphoreType.DMA((4,)),
        ],
        compiler_params=pltpu.CompilerParams(vmem_limit_bytes=VMEM_BYTES),
        name="between",
    )(gram, proj, raw, ensemble, cells)
    gram, proj = pl.pallas_call(
        second_kernel,
        out_shape=(shape(N, N), shape(1, N)),
        in_specs=[VM, VM, VM] + [SM] * 6,
        out_specs=(VM, VM),
        scratch_shapes=[pltpu.VMEM((RIM, 1, N), F32)] + exchange_scratch() + exchange_sems(),
        compiler_params=pltpu.CompilerParams(collective_id=1, has_side_effects=True, vmem_limit_bytes=VMEM_BYTES),
        name="second",
    )(rows, sides, held, *small)
    chunks = ROWS * COLS // CHUNK
    out = pl.pallas_call(
        last_kernel,
        out_shape=shape(ROWS * COLS, N),
        in_specs=[VM, VM, VM, ANY],
        out_specs=ANY,
        scratch_shapes=[
            pltpu.VMEM((ROWS * COLS, N), F32),
            pltpu.VMEM((ROWS * COLS, N), F32),
            pltpu.SemaphoreType.DMA((chunks,)),
            pltpu.SemaphoreType.DMA((chunks,)),
        ],
        compiler_params=pltpu.CompilerParams(vmem_limit_bytes=VMEM_BYTES),
        name="last",
    )(gram, proj, tt, ensemble.reshape(ROWS * COLS, N))
    return out.reshape(ROWS, COLS, N)


def solution(mesh):
    placed = (
        P("lat", "lon", None),
        P(None, "lat", "lon", None),
        P(None, "lat", "lon", None),
        P(None, "lat", "lon", None, None),
        P(None, "lat", "lon", None, None),
        P(None, "lat", "lon", None),
        P(None, "lat", "lon", None, None),
    )
    return jax.shard_map(
        local, mesh=mesh, in_specs=placed, out_specs=P("lat", "lon", None), check_vma=False
    )
```

```python
import functools
import math
import jax
import jax.numpy as jnp
from jax import lax
from jax.experimental import pallas as pl
from jax.experimental.pallas import tpu as pltpu
from jax.sharding import PartitionSpec as P

MESH = pl.DeviceIdType.MESH
F32 = jnp.float32
BF16 = jnp.bfloat16
ROWS, COLS, N = 32, 128, 128
SLOTS = 8
LATS, LONS = 24, 32
YS, XS = 8, 4
TOP, BOTTOM, LEFT, RIGHT, BLANK = 0, COLS + 2, 2 * (COLS + 2), 2 * (COLS + 2) + ROWS, 2 * (COLS + 2) + 2 * ROWS
RIM = BLANK + 1
NB = N // 8
NEAR = (-2, -1, 1, 2)
SLOT = sorted(
    ((dx, dy) for dx in (-1, 0, 1, 2) for dy in (-3, -2, -1, 0, 1, 2, 3, 4)), key=lambda p: (abs(p[0]) + abs(p[1]), p)
)
HOPS = [abs(dx) + abs(dy) for dx, dy in SLOT]
CUTS = (0, sum(h <= 2 for h in HOPS), sum(h <= 3 for h in HOPS), sum(h <= 4 for h in HOPS), LONS)
GROUPS = tuple(zip(CUTS[:-1], CUTS[1:]))
VMEM_BYTES = 48 * 2**20


def split3(x):
    high = x.astype(BF16).astype(F32)
    rest = x - high
    mid = rest.astype(BF16).astype(F32)
    return high, mid, rest - mid


def outer8(r, g):
    rh, rm, rl = split3(r)
    gh, gm, gl = split3(g)
    lhs = jnp.concatenate([rh, rh, rm, rh, rl, rm], axis=0).astype(BF16)
    rhs = jnp.concatenate([gh, gm, gh, gl, gh, gm], axis=0).astype(BF16)
    return lax.dot_general(lhs, rhs, (((0,), (0,)), ((), ())), preferred_element_type=F32)


def spread_row(x, k):
    return jnp.broadcast_to(x[k : k + 1, :], (8, N))


def spread_col(x, c):
    return jnp.broadcast_to(x[:, c : c + 1], (8, N))


def transform_t(gram, proj):
    lane = lax.broadcasted_iota(jnp.int32, (8, N), 1)
    sub = lax.broadcasted_iota(jnp.int32, (8, N), 0)
    prow = jnp.broadcast_to(proj, (8, N))
    w = [gram[8 * i : 8 * i + 8, :] + jnp.where(lane == sub + 8 * i, N - 1.0, 0.0) for i in range(NB)]
    inverse, sums = [], []
    acc = jnp.zeros((8, N), F32)
    for j in range(NB):
        c0 = 8 * j
        wj = w[j]
        cols = [spread_col(wj, c0 + k) for k in range(8)]
        here = (lane >= c0) & (lane < c0 + 8)
        f = jnp.where(here, jnp.where(lane == sub + c0, 1.0, 0.0), wj)
        lower, diag = f, cols[0]
        for k in range(8):
            inv = 1.0 / spread_row(cols[k], k)
            if k:
                lower = jnp.where(sub == k, f, lower)
                diag = jnp.where(sub == k, cols[k], diag)
            m = jnp.where(sub == k, 0.0, cols[k] * inv)
            for t in range(k + 1, 8):
                cols[t] = cols[t] - m * spread_row(cols[t], k)
            f = f - m * spread_row(f, k)
        g = f * (1.0 / diag)
        lj = jnp.where(lane <= c0 + 7, lower * lax.rsqrt(diag), 0.0)
        inverse.append(lj)
        sums.append(jnp.sum(lj, axis=1, keepdims=True))
        acc = acc + lj * jnp.sum(lj * prow, axis=1, keepdims=True)
        if j < NB - 1:
            nxt = w[j + 1]
            upd = jnp.where(here, 0.0, nxt)
            for k in range(8):
                upd = upd - spread_col(nxt, c0 + k) * spread_row(g, k)
            if j < NB - 2:
                p = outer8(wj, g)
                for i in range(j + 2, NB):
                    w[i] = jnp.where(here, 0.0, w[i]) - p[8 * i : 8 * i + 8, :]
            w[j + 1] = upd
    weights = jnp.sum(acc, axis=0, keepdims=True)
    total = jnp.sum(weights, axis=1, keepdims=True)
    root = math.sqrt(N - 1.0)
    out = []
    for i in range(NB):
        fix = (1.0 - (root * sums[i] + total)) * (1.0 / N)
        out.append(root * inverse[i] + weights + fix)
    return jnp.concatenate(out, axis=0)


def times(x, tt):
    return lax.dot_general(
        x, tt, (((1,), (1,)), ((), ())), precision=lax.Precision.HIGHEST, preferred_element_type=F32
    )


def position():
    lat, lon = lax.axis_index("lat"), lax.axis_index("lon")
    return lat, lon, lon // YS, lax.rem(lon, YS)


def inside(lat, step):
    return (lat + step >= 0) & (lat + step < LATS)


def east_west(lon):
    return lax.rem(lon + 1, LONS), lax.rem(lon + LONS - 1, LONS)


def lon_at(x, y, dx, dy):
    return lax.rem(x + dx + XS, XS) * YS + lax.rem(y + dy + YS, YS)


def enter(pos):
    lat, lon, x, y = pos
    barrier = pltpu.get_barrier_semaphore()

    def greet(a, c):
        pl.semaphore_signal(barrier, inc=1, device_id=(a, c), device_id_type=MESH)

    east, west = east_west(lon)
    for step in NEAR:

        @pl.when(inside(lat, step))
        def _():
            greet(lat + step, lon)
            if abs(step) == 1:
                greet(lat + step, east)
                greet(lat + step, west)

    greet(lat, east)
    greet(lat, west)
    for dx, dy in SLOT[:0:-1]:
        greet(lat, lon_at(x, y, -dx, -dy))
    count = LONS - 1 + 2
    for step in NEAR:
        count = count + jnp.where(inside(lat, step), 3 if abs(step) == 1 else 1, 0)
    pl.semaphore_wait(barrier, count)


def masks(pos, batch, pattern_ref, mark, markv):
    lat, lon, x, y = pos

    @pl.loop(0, 5)
    def _(d):
        for i, (dx, dy) in enumerate(SLOT):
            value = pattern_ref[batch, d, 0, lon_at(x, y, dx, dy)].astype(F32)
            mark[d, i] = jnp.full((SLOTS, N), value, F32).astype(BF16)
            markv[d, i] = jnp.full((1, N), value, F32)


def observe(batch, prior, observed_ref, precision_ref, owned_ref):
    sub = lax.broadcasted_iota(jnp.int32, (SLOTS, N), 0)
    obs = jnp.zeros((SLOTS, N), F32)
    prec = jnp.zeros((SLOTS, N), F32)
    own = jnp.zeros((SLOTS, N), F32)
    for o in range(SLOTS):
        obs = jnp.where(sub == o, observed_ref[batch, 0, o], obs)
        prec = jnp.where(sub == o, precision_ref[batch, 0, o], prec)
        own = jnp.where(sub == o, owned_ref[batch, 0, o].astype(F32), own)
    root = jnp.sqrt(prec) * own
    mean = jnp.sum(prior, axis=1, keepdims=True) * (1.0 / N)
    scaled = (root * (prior - mean)).astype(BF16)
    innov = (root * (obs - mean)).astype(BF16)
    vector = jnp.sum(scaled.astype(F32) * innov.astype(F32), axis=0, keepdims=True)
    return scaled, vector


class Exchange:
    def __init__(self, pos, seen, seenv, sems):
        self.pos, self.refs, self.sems = pos, (seen, seenv), (sems.at[0], sems.at[1])

    def pair(self, src, size, dst, device, send, recv):
        (sd, si), (dd, di) = src, dst
        return [
            pltpu.make_async_remote_copy(
                src_ref=ref.at[sd, pl.ds(si, size)], dst_ref=ref.at[dd, pl.ds(di, size)],
                send_sem=sem.at[send], recv_sem=sem.at[recv], device_id=device, device_id_type=MESH,
            )
            for ref, sem in zip(self.refs, self.sems)
        ]

    def blank(self):
        lat = self.pos[0]
        for step in NEAR:

            @pl.when(jnp.logical_not(inside(lat, step)))
            def _():
                for ref in self.refs:
                    ref[step + 2] = jnp.zeros(ref.shape[1:], ref.dtype)

    def row(self, i, g):
        lat, _, x, y = self.pos
        dx, dy = SLOT[i]
        return self.pair((2, 0), 1, (2, i), (lat, lon_at(x, y, -dx, -dy)), 0, 1 + g)

    def row_group(self, g):
        start, stop = max(GROUPS[g][0], 1), GROUPS[g][1]
        return self.pair((2, start), stop - start, (2, start), self.pos[:2], 0, 1 + g)

    def relay(self, k, start, stop):
        lat, lon = self.pos[:2]
        send = 1 + len(GROUPS) + k
        return self.pair(
            (2, start), stop - start, (2 - NEAR[k], start), (lat + NEAR[k], lon), send, send + len(NEAR)
        )

    def start(self, scaled, vector):
        self.refs[0][2, 0] = scaled
        self.refs[1][2, 0] = vector
        for g, (start, stop) in reversed(tuple(enumerate(GROUPS))):
            for i in reversed(range(max(start, 1), stop)):
                for c in self.row(i, g):
                    c.start()

    def finish(self, mark, markv):
        lat = self.pos[0]
        seen, seenv = self.refs

        def term(d):
            rows = seen[d]
            marked = rows * mark[d]
            gram = lax.dot_general(
                marked.reshape(LONS * SLOTS, N),
                rows.reshape(LONS * SLOTS, N),
                (((0,), (0,)), ((), ())),
                preferred_element_type=F32,
            )
            return gram, jnp.sum(seenv[d] * markv[d], axis=0)

        for g, (start, stop) in enumerate(GROUPS):
            for c in self.row_group(g):
                c.wait_recv()
            for k, step in enumerate(NEAR):

                @pl.when(inside(lat, step))
                def _():
                    for c in self.relay(k, start, stop):
                        c.start()

        gram, proj = term(2)
        for k, step in enumerate(NEAR):

            @pl.when(inside(lat, -step))
            def _():
                for c in self.relay(k, 0, LONS):
                    c.wait_recv()

            more, morev = term(2 - step)
            gram, proj = gram + more, proj + morev
        return gram, proj

    def drain(self):
        for c in self.pair((2, 1), LONS - 1, (2, 1), self.pos[:2], 0, 1):
            c.wait_send()
        for k, step in enumerate(NEAR):

            @pl.when(inside(self.pos[0], step))
            def _():
                for c in self.relay(k, 0, LONS):
                    c.wait_send()


class Halo:
    def __init__(self, pos, sems, rows, ends, sides, targets):
        self.pos, self.sems, self.rows, self.ends, self.sides, self.targets = pos, sems, rows, ends, sides, targets

    def copy(self, src, dst, recv, device):
        return pltpu.make_async_remote_copy(
            src_ref=src, dst_ref=dst, send_sem=self.sems.at[recv], recv_sem=self.sems.at[4 + recv],
            device_id=device, device_id_type=MESH,
        )

    def across(self):
        lat, lon = self.pos[:2]
        east, west = east_west(lon)
        left, right = self.targets["sides"]
        return [self.copy(self.sides[1], left, 0, (lat, east)), self.copy(self.sides[0], right, 1, (lat, west))]

    def along(self, step):
        lat, lon = self.pos[:2]
        east, west = east_west(lon)
        which, to = (1, 0) if step == 1 else (0, 1)
        row, first, last, _ = self.targets["rows"][to]
        return [
            self.copy(self.ends[which][1], first, 2 + to, (lat + step, east)),
            self.copy(self.ends[which][0], last, 2 + to, (lat + step, west)),
            self.copy(self.rows[which], row, 2 + to, (lat + step, lon)),
        ]

    def whole(self, step):
        to = 0 if step == 1 else 1
        row = self.targets["rows"][to][3]
        return self.copy(row, row, 2 + to, self.pos[:2])

    def start(self):
        for step in (1, -1):

            @pl.when(inside(self.pos[0], step))
            def _():
                for c in self.along(step):
                    c.start()

        for c in self.across():
            c.start()

    def arrive(self):
        for c in self.across():
            c.wait_recv()
        for step in (1, -1):

            @pl.when(inside(self.pos[0], -step))
            def _():
                self.whole(step).wait_recv()

    def drain(self):
        for c in self.across():
            c.wait_send()
        for step in (1, -1):

            @pl.when(inside(self.pos[0], step))
            def _():
                self.whole(step).wait_send()


def corner(stencil_ref, batch, o):
    s = stencil_ref[batch, 0, o]
    r = s // (COLS + 2)
    return r, s - r * (COLS + 2)


def main_kernel(
    cells, ens, observed_in, precision_in, weight_in, stencil_in, owned_in, pattern_in,
    gram_ref, proj_ref, tt_ref,
    observed, precision, weight, stencil, owned, pattern,
    tile, rim, edge, strip, edge_out, strip_out, prior, held,
    seen0, seenv0, seen1, seenv1, mark, markv,
    small_sem, local_sem, halo0_sem, halo1_sem, sem0, sem1,
):
    pos = position()
    lat, lon, x, y = pos
    smalls = [
        pltpu.make_async_copy(src, dst, small_sem.at[i])
        for i, (src, dst) in enumerate(
            (
                (observed_in, observed),
                (precision_in, precision),
                (weight_in, weight),
                (stencil_in, stencil),
                (owned_in, owned),
                (pattern_in, pattern),
            )
        )
    ]
    inner = pltpu.make_async_copy(cells, tile.at[pl.ds(1, ROWS), pl.ds(1, COLS)], local_sem.at[0])
    edges = [
        pltpu.make_async_copy(ens.at[0], edge.at[0], local_sem.at[1]),
        pltpu.make_async_copy(ens.at[ROWS - 1], edge.at[1], local_sem.at[2]),
        pltpu.make_async_copy(cells.at[:, 0], strip.at[0], local_sem.at[3]),
        pltpu.make_async_copy(cells.at[:, COLS - 1], strip.at[1], local_sem.at[4]),
    ]
    for c in smalls + [inner] + edges:
        c.start()
    first = Exchange(pos, seen0, seenv0, sem0)
    second = Exchange(pos, seen1, seenv1, sem1)
    first.blank()
    second.blank()
    rim[BLANK] = jnp.zeros((1, N), F32)
    for step, r, to in ((-1, 0, TOP), (1, ROWS + 1, BOTTOM)):

        @pl.when(jnp.logical_not(inside(lat, step)))
        def _():
            tile[r] = jnp.zeros((COLS + 2, 1, N), F32)
            rim[pl.ds(to, COLS + 2)] = jnp.zeros((COLS + 2, 1, N), F32)

    enter(pos)

    halo = Halo(
        pos,
        halo0_sem,
        rows=(cells.at[0], cells.at[ROWS - 1]),
        ends=((cells.at[0, 0], cells.at[0, COLS - 1]), (cells.at[ROWS - 1, 0], cells.at[ROWS - 1, COLS - 1])),
        sides=(cells.at[:, 0], cells.at[:, COLS - 1]),
        targets={
            "sides": (tile.at[pl.ds(1, ROWS), 0], tile.at[pl.ds(1, ROWS), COLS + 1]),
            "rows": tuple(
                (tile.at[r, pl.ds(1, COLS)], tile.at[r, 0], tile.at[r, COLS + 1], tile.at[r]) for r in (0, ROWS + 1)
            ),
        },
    )
    halo.start()
    for c in smalls:
        c.wait()
    masks(pos, 0, pattern, mark.at[0], markv.at[0])
    inner.wait()
    halo.arrive()

    for o in range(SLOTS):
        r, c = corner(stencil, 0, o)
        total = jnp.zeros((1, N), F32)
        for k in range(4):
            total = total + weight[0, k, o] * tile[r + k // 2, c + k % 2]
        prior[pl.ds(o, 1), :] = total
    first.start(*observe(0, prior[...], observed, precision, owned))
    for o in range(SLOTS):
        r, c = corner(stencil, 1, o)
        total = jnp.zeros((1, N), F32)
        for k in range(4):
            rk, ck = r + k // 2, c + k % 2
            own = (rk >= 1) & (rk <= ROWS) & (ck >= 1) & (ck <= COLS)
            total = total + jnp.where(own, weight[1, k, o], 0.0) * tile[rk, ck]
        held[pl.ds(o, 1), :] = total
    masks(pos, 1, pattern, mark.at[1], markv.at[1])
    for c in edges:
        c.wait()
    gram, proj = first.finish(mark.at[0], markv.at[0])

    tt = transform_t(gram, proj)
    for i in range(2):
        edge_out[i] = times(edge[i], tt).reshape(COLS, 1, N)
        strip_out[i] = times(strip[i].reshape(ROWS, N), tt).reshape(ROWS, 1, N)
    halo2 = Halo(
        pos,
        halo1_sem,
        rows=(edge_out.at[0], edge_out.at[1]),
        ends=tuple((edge_out.at[i, pl.ds(0, 1)], edge_out.at[i, pl.ds(COLS - 1, 1)]) for i in range(2)),
        sides=(strip_out.at[0], strip_out.at[1]),
        targets={
            "sides": (rim.at[pl.ds(LEFT, ROWS)], rim.at[pl.ds(RIGHT, ROWS)]),
            "rows": tuple(
                (
                    rim.at[pl.ds(to + 1, COLS)],
                    rim.at[pl.ds(to, 1)],
                    rim.at[pl.ds(to + COLS + 1, 1)],
                    rim.at[pl.ds(to, COLS + 2)],
                )
                for to in (TOP, BOTTOM)
            ),
        },
    )
    halo2.start()
    tt_ref[...] = tt
    prior[...] = times(held[...], tt)
    halo2.arrive()
    for o in range(SLOTS):
        r, c = corner(stencil, 1, o)
        total = prior[pl.ds(o, 1), :]
        for k in range(4):
            rk, ck = r + k // 2, c + k % 2
            where = jnp.where(ck == 0, LEFT - 1 + rk, jnp.where(ck == COLS + 1, RIGHT - 1 + rk, BLANK))
            where = jnp.where(rk == 0, TOP + ck, jnp.where(rk == ROWS + 1, BOTTOM + ck, where))
            total = total + weight[1, k, o] * rim[where]
        prior[pl.ds(o, 1), :] = total
    second.start(*observe(1, prior[...], observed, precision, owned))
    gram_ref[...], proj_ref[...] = second.finish(mark.at[1], markv.at[1])
    halo.drain()
    first.drain()
    halo2.drain()
    second.drain()


CHUNK = 512


def last_kernel(gram, proj, tt_ref, ens, out, cells, moved, in_sem, out_sem):
    chunks = ROWS * COLS // CHUNK
    loads = [
        pltpu.make_async_copy(ens.at[pl.ds(i * CHUNK, CHUNK)], cells.at[pl.ds(i * CHUNK, CHUNK)], in_sem.at[i])
        for i in range(chunks)
    ]
    for c in loads:
        c.start()
    tt = transform_t(gram[...], proj[...])
    both = jnp.dot(tt, tt_ref[...], precision=lax.Precision.HIGHEST, preferred_element_type=F32)
    high = both.astype(BF16)
    low = (both - high.astype(F32)).astype(BF16)
    right = jnp.concatenate(
        [jnp.concatenate([high, high], axis=1), jnp.concatenate([low, jnp.zeros_like(low)], axis=1)], axis=0
    )
    stores = []
    for i in range(chunks):
        rows = pl.ds(i * CHUNK, CHUNK)
        loads[i].wait()
        xs = cells[rows, :]
        xh = xs.astype(BF16)
        xl = (xs - xh.astype(F32)).astype(BF16)
        res = lax.dot_general(
            jnp.concatenate([xh, xl], axis=1), right, (((1,), (1,)), ((), ())), preferred_element_type=F32
        )
        moved[rows, :] = res[:, :N] + res[:, N:]
        c = pltpu.make_async_copy(moved.at[rows], out.at[rows], out_sem.at[i])
        c.start()
        stores.append(c)
    for c in stores:
        c.wait()


def shape(*dims):
    return jax.ShapeDtypeStruct(dims, F32)


VM = pl.BlockSpec(memory_space=pltpu.VMEM)
HBM = pl.BlockSpec(memory_space=pltpu.HBM)


def local(ensemble, observed, precision, interp_weight, stencil, owned, pattern):
    cells = ensemble.reshape(ROWS, COLS, 1, N)
    small = (
        observed.reshape(2, 1, SLOTS),
        precision.reshape(2, 1, SLOTS),
        interp_weight.reshape(2, 4, SLOTS),
        stencil.reshape(2, 4, SLOTS),
        owned.reshape(2, 1, SLOTS),
        pattern.transpose(0, 1, 3, 2, 4).reshape(2, 5, 1, LONS),
    )
    blocks = [pltpu.VMEM((5, LONS, SLOTS, N), BF16), pltpu.VMEM((5, LONS, 1, N), F32)]
    gram, proj, tt = pl.pallas_call(
        main_kernel,
        out_shape=(shape(N, N), shape(1, N), shape(N, N)),
        in_specs=[HBM] * 8,
        out_specs=(VM, VM, VM),
        scratch_shapes=[pltpu.SMEM(a.shape, a.dtype) for a in small]
        + [
            pltpu.VMEM((ROWS + 2, COLS + 2, 1, N), F32),
            pltpu.VMEM((RIM, 1, N), F32),
            pltpu.VMEM((2, COLS, N), F32),
            pltpu.VMEM((2, ROWS, 1, N), F32),
            pltpu.VMEM((2, COLS, 1, N), F32),
            pltpu.VMEM((2, ROWS, 1, N), F32),
            pltpu.VMEM((SLOTS, N), F32),
            pltpu.VMEM((SLOTS, N), F32),
        ]
        + blocks
        + blocks
        + [pltpu.VMEM((2, 5, LONS, SLOTS, N), BF16), pltpu.VMEM((2, 5, LONS, 1, N), F32)]
        + [pltpu.SemaphoreType.DMA((len(small),)), pltpu.SemaphoreType.DMA((5,))]
        + [pltpu.SemaphoreType.DMA((8,))] * 2
        + [pltpu.SemaphoreType.DMA((2, 1 + len(GROUPS) + 2 * len(NEAR)))] * 2,
        compiler_params=pltpu.CompilerParams(collective_id=0, has_side_effects=True, vmem_limit_bytes=VMEM_BYTES),
        name="main",
    )(*(pltpu.with_memory_space_constraint(a, pltpu.HBM) for a in (cells, ensemble) + small))
    chunks = ROWS * COLS // CHUNK
    out = pl.pallas_call(
        last_kernel,
        out_shape=shape(ROWS * COLS, N),
        in_specs=[VM, VM, VM, HBM],
        out_specs=HBM,
        scratch_shapes=[
            pltpu.VMEM((ROWS * COLS, N), F32),
            pltpu.VMEM((ROWS * COLS, N), F32),
            pltpu.SemaphoreType.DMA((chunks,)),
            pltpu.SemaphoreType.DMA((chunks,)),
        ],
        compiler_params=pltpu.CompilerParams(vmem_limit_bytes=VMEM_BYTES),
        name="last",
    )(gram, proj, tt, pltpu.with_memory_space_constraint(ensemble.reshape(ROWS * COLS, N), pltpu.HBM))
    return out.reshape(ROWS, COLS, N)


def solution(mesh):
    placed = (
        P("lat", "lon", None),
        P(None, "lat", "lon", None),
        P(None, "lat", "lon", None),
        P(None, "lat", "lon", None, None),
        P(None, "lat", "lon", None, None),
        P(None, "lat", "lon", None),
        P(None, "lat", "lon", None, None),
    )
    return jax.shard_map(
        local, mesh=mesh, in_specs=placed, out_specs=P("lat", "lon", None), check_vma=False
    )
```

```python
import functools
import math
import jax
import jax.numpy as jnp
from jax import lax
from jax.experimental import pallas as pl
from jax.experimental.pallas import tpu as pltpu
from jax.sharding import PartitionSpec as P

MESH = pl.DeviceIdType.MESH
F32 = jnp.float32
BF16 = jnp.bfloat16
ROWS, COLS, N = 32, 128, 128
SLOTS = 8
LATS, LONS = 24, 32
YS, XS = 8, 4
AROUND = ((-1, -1), (-1, 0), (-1, 1), (0, -1), (0, 1), (1, -1), (1, 0), (1, 1))
THIRDS = ((0, 3, -1), (3, 5, 0), (5, 8, 1))
NB = N // 8
NEAR = (-2, -1, 1, 2)
OWN = len(NEAR)
SLOT = sorted(
    ((dx, dy) for dx in (-1, 0, 1, 2) for dy in (-3, -2, -1, 0, 1, 2, 3, 4)), key=lambda p: (abs(p[0]) + abs(p[1]), p)
)
HOPS = [abs(dx) + abs(dy) for dx, dy in SLOT]
CUTS = (0, sum(h <= 2 for h in HOPS), sum(h <= 3 for h in HOPS), sum(h <= 4 for h in HOPS), LONS)
GROUPS = tuple(zip(CUTS[:-1], CUTS[1:]))
PAIRS = SLOTS // 2 + 1
VMEM_BYTES = 48 * 2**20


def split3(x):
    high = x.astype(BF16).astype(F32)
    rest = x - high
    mid = rest.astype(BF16).astype(F32)
    return high, mid, rest - mid


def outer8(r, g):
    rh, rm, rl = split3(r)
    gh, gm, gl = split3(g)
    lhs = jnp.concatenate([rh, rh, rm, rh, rl, rm], axis=0).astype(BF16)
    rhs = jnp.concatenate([gh, gm, gh, gl, gh, gm], axis=0).astype(BF16)
    return lax.dot_general(lhs, rhs, (((0,), (0,)), ((), ())), preferred_element_type=F32)


def spread_row(x, k):
    return jnp.broadcast_to(x[k : k + 1, :], (8, N))


def spread_col(x, c):
    return jnp.broadcast_to(x[:, c : c + 1], (8, N))


def transform_t(gram, proj):
    lane = lax.broadcasted_iota(jnp.int32, (8, N), 1)
    sub = lax.broadcasted_iota(jnp.int32, (8, N), 0)
    prow = jnp.broadcast_to(proj, (8, N))
    w = [gram[8 * i : 8 * i + 8, :] + jnp.where(lane == sub + 8 * i, N - 1.0, 0.0) for i in range(NB)]
    inverse, sums = [], []
    acc = jnp.zeros((8, N), F32)
    for j in range(NB):
        c0 = 8 * j
        wj = w[j]
        cols = [spread_col(wj, c0 + k) for k in range(8)]
        here = (lane >= c0) & (lane < c0 + 8)
        f = jnp.where(here, jnp.where(lane == sub + c0, 1.0, 0.0), wj)
        for k in range(8):
            d = spread_row(cols[k], k)
            below = jnp.where(sub == k, 0.0, cols[k])
            inv = 1.0 / d
            if k:
                lower = jnp.where(sub == k, f, lower)
                diag = jnp.where(sub == k, d, diag)
                inverse_diag = jnp.where(sub == k, inv, inverse_diag)
            else:
                lower, diag, inverse_diag = f, d, inv
            for t in range(k + 1, 8):
                cols[t] = cols[t] - (below * spread_row(cols[t], k)) * inv
            f = f - (below * spread_row(f, k)) * inv
        g = f * inverse_diag
        lj = jnp.where(lane <= c0 + 7, lower * lax.rsqrt(diag), 0.0)
        inverse.append(lj)
        sums.append(jnp.sum(lj, axis=1, keepdims=True))
        acc = acc + lj * jnp.sum(lj * prow, axis=1, keepdims=True)
        if j < NB - 1:
            nxt = w[j + 1]
            terms = [spread_col(nxt, c0 + k) * spread_row(g, k) for k in range(8)]
            while len(terms) > 1:
                terms = [a + b for a, b in zip(terms[::2], terms[1::2])]
            upd = jnp.where(here, 0.0, nxt) - terms[0]
            if j < NB - 2:
                p = outer8(wj, g)
                for i in range(j + 2, NB):
                    w[i] = jnp.where(here, 0.0, w[i]) - p[8 * i : 8 * i + 8, :]
            w[j + 1] = upd
    weights = jnp.sum(acc, axis=0, keepdims=True)
    total = jnp.sum(weights, axis=1, keepdims=True)
    root = math.sqrt(N - 1.0)
    out = []
    for i in range(NB):
        fix = (1.0 - (root * sums[i] + total)) * (1.0 / N)
        out.append(root * inverse[i] + weights + fix)
    return jnp.concatenate(out, axis=0)


def times(x, tt):
    return lax.dot_general(
        x, tt, (((1,), (1,)), ((), ())), precision=lax.Precision.HIGHEST, preferred_element_type=F32
    )


def position():
    lat, lon = lax.axis_index("lat"), lax.axis_index("lon")
    return lat, lon, lon // YS, lax.rem(lon, YS)


def inside(lat, step):
    return (lat + step >= 0) & (lat + step < LATS)


def east_west(lon):
    return lax.rem(lon + 1, LONS), lax.rem(lon + LONS - 1, LONS)


def lon_at(x, y, dx, dy):
    return lax.rem(x + dx + XS, XS) * YS + lax.rem(y + dy + YS, YS)


def announce(pos):
    lat, lon, x, y = pos
    barrier = pltpu.get_barrier_semaphore()

    def greet(a, c):
        pl.semaphore_signal(barrier, inc=1, device_id=(a, c), device_id_type=MESH)

    east, west = east_west(lon)
    for step in NEAR:

        @pl.when(inside(lat, step))
        def _():
            greet(lat + step, lon)
            if abs(step) == 1:
                greet(lat + step, east)
                greet(lat + step, west)

    greet(lat, east)
    greet(lat, west)
    for dx, dy in SLOT[:0:-1]:
        greet(lat, lon_at(x, y, -dx, -dy))


def enter(pos):
    lat = pos[0]
    count = LONS - 1 + 2
    for step in NEAR:
        count = count + jnp.where(inside(lat, step), 3 if abs(step) == 1 else 1, 0)
    pl.semaphore_wait(pltpu.get_barrier_semaphore(), count)


def masks(pos, batch, pattern_ref, mark, markv, pick):
    lat, lon, x, y = pos

    @pl.loop(0, OWN + 1)
    def _(d):
        line = jnp.where(d == OWN, 2, jnp.where(d < 2, d, d + 1))
        for i, (dx, dy) in enumerate(SLOT):
            value = pattern_ref[batch, line, 0, lon_at(x, y, dx, dy)].astype(F32)
            both = jnp.full((PAIRS - 1, 2, N), value, F32).astype(BF16)
            mark[d, i, pl.ds(0, PAIRS - 1)] = both
            mark[d, i, PAIRS - 1] = jnp.zeros((2, N), BF16)
            markv[d, i, pl.ds(0, PAIRS - 1)] = jnp.zeros((PAIRS - 1, 2, N), BF16)
            markv[d, i, PAIRS - 1] = both[0]

    first = (lax.broadcasted_iota(jnp.int32, (16, N), 1) == 0).astype(F32).astype(BF16)
    for d in range(OWN + 1):
        pick[d] = lax.dot_general(
            first, markv[d].reshape(LONS * PAIRS * 2, N), (((1,), (1,)), ((), ())), preferred_element_type=F32
        ).astype(BF16)


def observe(batch, prior, observed_ref, precision_ref, owned_ref):
    sub = lax.broadcasted_iota(jnp.int32, (SLOTS, N), 0)
    obs = jnp.zeros((SLOTS, N), F32)
    prec = jnp.zeros((SLOTS, N), F32)
    own = jnp.zeros((SLOTS, N), F32)
    for o in range(SLOTS):
        obs = jnp.where(sub == o, observed_ref[batch, 0, o], obs)
        prec = jnp.where(sub == o, precision_ref[batch, 0, o], prec)
        own = jnp.where(sub == o, owned_ref[batch, 0, o].astype(F32), own)
    root = jnp.sqrt(prec) * own
    mean = jnp.sum(prior, axis=1, keepdims=True) * (1.0 / N)
    scaled = (root * (prior - mean)).astype(BF16)
    innov = (root * (obs - mean)).astype(BF16)
    vector = jnp.sum(scaled.astype(F32) * innov.astype(F32), axis=0, keepdims=True)
    return scaled, vector


class Exchange:
    def __init__(self, pos, seen, sems):
        self.pos, self.seen, self.sems = pos, seen, sems

    def copy(self, src, size, dst, device, send, recv):
        (sd, si), (dd, di) = src, dst
        return pltpu.make_async_remote_copy(
            src_ref=self.seen.at[sd, pl.ds(si, size)], dst_ref=self.seen.at[dd, pl.ds(di, size)],
            send_sem=self.sems.at[send], recv_sem=self.sems.at[recv], device_id=device, device_id_type=MESH,
        )

    def blank(self):
        for step in NEAR:

            @pl.when(jnp.logical_not(inside(self.pos[0], step)))
            def _():
                self.seen[NEAR.index(step)] = jnp.zeros(self.seen.shape[1:], BF16)

    def row(self, i, g):
        lat, _, x, y = self.pos
        dx, dy = SLOT[i]
        return self.copy((OWN, 0), 1, (OWN, i), (lat, lon_at(x, y, -dx, -dy)), 0, 1 + g)

    def row_group(self, g):
        start, stop = max(GROUPS[g][0], 1), GROUPS[g][1]
        return self.copy((OWN, start), stop - start, (OWN, start), self.pos[:2], 0, 1 + g)

    def relay(self, k, start, stop):
        lat, lon = self.pos[:2]
        send = 1 + len(GROUPS) + k
        return self.copy(
            (OWN, start), stop - start, (OWN - 1 - k, start), (lat + NEAR[k], lon), send, send + len(NEAR)
        )

    def start(self, scaled, vector):
        for i in range(PAIRS - 1):
            self.seen[OWN, 0, i] = scaled[2 * i : 2 * i + 2, :]
        high = vector.astype(BF16)
        self.seen[OWN, 0, PAIRS - 1] = jnp.concatenate([high.astype(F32), vector - high.astype(F32)], axis=0).astype(BF16)
        for g, (start, stop) in reversed(tuple(enumerate(GROUPS))):
            for i in reversed(range(max(start, 1), stop)):
                self.row(i, g).start()

    def finish(self, mark, pick):
        lat = self.pos[0]

        def term(d, size):
            flat = self.seen[pl.ds(d, size)].reshape(size * LONS * PAIRS * 2, N)
            marked = flat * mark[pl.ds(d, size)].reshape(size * LONS * PAIRS * 2, N)
            gram = lax.dot_general(marked, flat, (((0,), (0,)), ((), ())), preferred_element_type=F32)
            proj = jnp.zeros((16, N), F32)
            for i in range(size):
                rows = flat[i * LONS * PAIRS * 2 : (i + 1) * LONS * PAIRS * 2]
                proj = proj + jnp.dot(pick[d + i], rows, preferred_element_type=F32)
            return gram, proj[0:1]

        for g, (start, stop) in enumerate(GROUPS):
            self.row_group(g).wait_recv()
            for k, step in enumerate(NEAR):

                @pl.when(inside(lat, step))
                def _():
                    self.relay(k, start, stop).start()

        gram, proj = term(OWN, 1)
        for k, step in enumerate(NEAR):

            @pl.when(inside(lat, -step))
            def _():
                self.relay(k, 0, LONS).wait_recv()

        more, morev = term(0, OWN)
        return gram + more, proj + morev

    def drain(self):
        self.copy((OWN, 1), LONS - 1, (OWN, 1), self.pos[:2], 0, 1).wait_send()
        for k, step in enumerate(NEAR):

            @pl.when(inside(self.pos[0], step))
            def _():
                self.relay(k, 0, LONS).wait_send()


class Around:
    def __init__(self, pos, src, dst, sems):
        self.pos, self.src, self.dst, self.sems = pos, src, dst, sems

    def copies(self, g):
        lat, lon = self.pos[:2]
        start, stop, step = THIRDS[g]
        return [
            pltpu.make_async_remote_copy(
                src_ref=self.src.at[n], dst_ref=self.dst.at[7 - n],
                send_sem=self.sems.at[g], recv_sem=self.sems.at[5 - g],
                device_id=(lat + step, lax.rem(lon + AROUND[n][1] + LONS, LONS)), device_id_type=MESH,
            )
            for n in range(start, stop)
        ]

    def group(self, g):
        start, stop, _ = THIRDS[g]
        return pltpu.make_async_remote_copy(
            src_ref=self.src.at[pl.ds(start, stop - start)], dst_ref=self.dst.at[pl.ds(start, stop - start)],
            send_sem=self.sems.at[g], recv_sem=self.sems.at[3 + g], device_id=self.pos[:2], device_id_type=MESH,
        )

    def each(self, act):
        for g, (_, _, step) in enumerate(THIRDS):
            if step == 0:
                act(g)
            else:
                pl.when(inside(self.pos[0], step))(functools.partial(act, g))

    def blank(self):
        for start, stop, step in THIRDS:

            @pl.when(jnp.logical_not(inside(self.pos[0], step)))
            def _():
                self.dst[pl.ds(start, stop - start)] = jnp.zeros((stop - start, SLOTS, N), F32)

    def start(self):
        def act(g):
            for c in self.copies(g):
                c.start()

        self.each(act)

    def arrive(self):
        self.each(lambda g: self.group(g).wait_recv())

    def drain(self):
        self.each(lambda g: self.group(g).wait_send())


class Halo:
    def __init__(self, pos, sems, rows, ends, sides, targets):
        self.pos, self.sems, self.rows, self.ends, self.sides, self.targets = pos, sems, rows, ends, sides, targets

    def copy(self, src, dst, recv, device):
        return pltpu.make_async_remote_copy(
            src_ref=src, dst_ref=dst, send_sem=self.sems.at[recv], recv_sem=self.sems.at[4 + recv],
            device_id=device, device_id_type=MESH,
        )

    def across(self):
        lat, lon = self.pos[:2]
        east, west = east_west(lon)
        left, right = self.targets["sides"]
        return [self.copy(self.sides[1], left, 0, (lat, east)), self.copy(self.sides[0], right, 1, (lat, west))]

    def along(self, step):
        lat, lon = self.pos[:2]
        east, west = east_west(lon)
        which, to = (1, 0) if step == 1 else (0, 1)
        row, first, last, _ = self.targets["rows"][to]
        return [
            self.copy(self.ends[which][1], first, 2 + to, (lat + step, east)),
            self.copy(self.ends[which][0], last, 2 + to, (lat + step, west)),
            self.copy(self.rows[which], row, 2 + to, (lat + step, lon)),
        ]

    def whole(self, step):
        to = 0 if step == 1 else 1
        row = self.targets["rows"][to][3]
        return self.copy(row, row, 2 + to, self.pos[:2])

    def start(self):
        for step in (1, -1):

            @pl.when(inside(self.pos[0], step))
            def _():
                for c in self.along(step):
                    c.start()

        for c in self.across():
            c.start()

    def arrive(self):
        for c in self.across():
            c.wait_recv()
        for step in (1, -1):

            @pl.when(inside(self.pos[0], -step))
            def _():
                self.whole(step).wait_recv()

    def drain(self):
        for c in self.across():
            c.wait_send()
        for step in (1, -1):

            @pl.when(inside(self.pos[0], step))
            def _():
                self.whole(step).wait_send()


def corner(stencil_ref, batch, o):
    s = stencil_ref[batch, 0, o]
    r = s // (COLS + 2)
    return r, s - r * (COLS + 2)


def main_kernel(
    cells, observed_in, precision_in, weight_in, stencil_in, owned_in, pattern_in,
    gram_ref, proj_ref, tt_ref,
    observed, precision, weight, stencil, owned, pattern,
    tile, prior, ask, asked, answer, answered, seen0, seen1, mark, markv, pick,
    small_sem, inner_sem, halo_sem, ask_sem, answer_sem, sem0, sem1,
):
    pos = position()
    lat = pos[0]
    announce(pos)
    inner = pltpu.make_async_copy(cells, tile.at[pl.ds(1, ROWS), pl.ds(1, COLS)], inner_sem)
    inner.start()
    smalls = [
        pltpu.make_async_copy(src, dst, small_sem.at[i])
        for i, (src, dst) in enumerate(
            (
                (pattern_in, pattern),
                (observed_in, observed),
                (precision_in, precision),
                (weight_in, weight),
                (stencil_in, stencil),
                (owned_in, owned),
            )
        )
    ]
    for c in smalls:
        c.start()
    first = Exchange(pos, seen0, sem0)
    second = Exchange(pos, seen1, sem1)
    asks = Around(pos, ask.at[pl.ds(0, 8)], asked, ask_sem)
    answers = Around(pos, answer, answered, answer_sem)
    for part in (first, second, asks, answers):
        part.blank()
    for step, r in ((-1, 0), (1, ROWS + 1)):

        @pl.when(jnp.logical_not(inside(lat, step)))
        def _():
            tile[r] = jnp.zeros((COLS + 2, 1, N), F32)

    halo = Halo(
        pos,
        halo_sem,
        rows=(tile.at[1, pl.ds(1, COLS)], tile.at[ROWS, pl.ds(1, COLS)]),
        ends=((tile.at[1, 1], tile.at[1, COLS]), (tile.at[ROWS, 1], tile.at[ROWS, COLS])),
        sides=(tile.at[pl.ds(1, ROWS), 1], tile.at[pl.ds(1, ROWS), COLS]),
        targets={
            "sides": (tile.at[pl.ds(1, ROWS), 0], tile.at[pl.ds(1, ROWS), COLS + 1]),
            "rows": tuple(
                (tile.at[r, pl.ds(1, COLS)], tile.at[r, 0], tile.at[r, COLS + 1], tile.at[r]) for r in (0, ROWS + 1)
            ),
        },
    )
    inner.wait()
    enter(pos)
    halo.start()
    for c in smalls:
        c.wait()
    masks(pos, 0, pattern, mark.at[0], markv, pick.at[0])
    halo.arrive()

    for o in range(SLOTS):
        r, c = corner(stencil, 0, o)
        total = jnp.zeros((1, N), F32)
        for k in range(4):
            total = total + weight[0, k, o] * tile[r + k // 2, c + k % 2]
        prior[pl.ds(o, 1), :] = total
    first.start(*observe(0, prior[...], observed, precision, owned))

    for o in range(SLOTS):
        r, c = corner(stencil, 1, o)
        shares = [jnp.zeros((1, N), F32) for _ in range(9)]
        for k in range(4):
            rk, ck = r + k // 2, c + k % 2
            up, down = rk == 0, rk == ROWS + 1
            left, right = ck == 0, ck == COLS + 1
            middle, centre = jnp.logical_not(up | down), jnp.logical_not(left | right)
            cell, scale = tile[rk, ck], weight[1, k, o]
            for n, (dr, dc) in enumerate(AROUND + ((0, 0),)):
                there = (up, middle, down)[dr + 1] & (left, centre, right)[dc + 1]
                shares[n] = shares[n] + jnp.where(there, scale, 0.0) * cell
        for n in range(9):
            ask[n, pl.ds(o, 1), :] = shares[n]
    asks.start()
    masks(pos, 1, pattern, mark.at[1], markv, pick.at[1])
    gram, proj = first.finish(mark.at[0], pick.at[0])
    asks.arrive()

    tt = transform_t(gram, proj)
    answer[...] = times(asked[...].reshape(8 * SLOTS, N), tt).reshape(8, SLOTS, N)
    answers.start()
    tt_ref[...] = tt
    total = times(ask[8], tt)
    answers.arrive()
    for n in range(8):
        total = total + answered[n]
    second.start(*observe(1, total, observed, precision, owned))
    gram_ref[...], proj_ref[...] = second.finish(mark.at[1], pick.at[1])
    for part in (halo, first, asks, answers, second):
        part.drain()


CHUNK = 1024


def last_kernel(gram, proj, tt_ref, ens, out, cells, moved, in_sem, out_sem):
    chunks = ROWS * COLS // CHUNK
    load = pltpu.make_async_copy(ens, cells, in_sem)
    load.start()
    tt = transform_t(gram[...], proj[...])
    both = jnp.dot(tt, tt_ref[...], precision=lax.Precision.HIGHEST, preferred_element_type=F32)
    high = both.astype(BF16)
    low = (both - high.astype(F32)).astype(BF16)
    right = jnp.concatenate(
        [jnp.concatenate([high, high], axis=1), jnp.concatenate([low, jnp.zeros_like(low)], axis=1)], axis=0
    )
    stores = []
    load.wait()
    for i in range(chunks):
        rows = pl.ds(i * CHUNK, CHUNK)
        xs = cells[rows, :]
        xh = xs.astype(BF16)
        xl = (xs - xh.astype(F32)).astype(BF16)
        res = lax.dot_general(
            jnp.concatenate([xh, xl], axis=1), right, (((1,), (1,)), ((), ())), preferred_element_type=F32
        )
        moved[rows, :] = res[:, :N] + res[:, N:]
        c = pltpu.make_async_copy(moved.at[rows], out.at[rows], out_sem.at[i])
        c.start()
        stores.append(c)
    for c in stores:
        c.wait()


def shape(*dims):
    return jax.ShapeDtypeStruct(dims, F32)


VM = pl.BlockSpec(memory_space=pltpu.VMEM)
HBM = pl.BlockSpec(memory_space=pltpu.HBM)


def local(ensemble, observed, precision, interp_weight, stencil, owned, pattern):
    cells = ensemble.reshape(ROWS, COLS, 1, N)
    small = (
        observed.reshape(2, 1, SLOTS),
        precision.reshape(2, 1, SLOTS),
        interp_weight.reshape(2, 4, SLOTS),
        stencil.reshape(2, 4, SLOTS),
        owned.reshape(2, 1, SLOTS),
        pattern.transpose(0, 1, 3, 2, 4).reshape(2, 5, 1, LONS),
    )
    gram, proj, tt = pl.pallas_call(
        main_kernel,
        out_shape=(shape(N, N), shape(1, N), shape(N, N)),
        in_specs=[HBM] * 7,
        out_specs=(VM, VM, VM),
        scratch_shapes=[pltpu.SMEM(a.shape, a.dtype) for a in small]
        + [
            pltpu.VMEM((ROWS + 2, COLS + 2, 1, N), F32),
            pltpu.VMEM((SLOTS, N), F32),
            pltpu.VMEM((9, SLOTS, N), F32),
            pltpu.VMEM((8, SLOTS, N), F32),
            pltpu.VMEM((8, SLOTS, N), F32),
            pltpu.VMEM((8, SLOTS, N), F32),
            pltpu.VMEM((5, LONS, PAIRS, 2, N), BF16),
            pltpu.VMEM((5, LONS, PAIRS, 2, N), BF16),
            pltpu.VMEM((2, 5, LONS, PAIRS, 2, N), BF16),
            pltpu.VMEM((5, LONS, PAIRS, 2, N), BF16),
            pltpu.VMEM((2, 5, 16, LONS * PAIRS * 2), BF16),
            pltpu.SemaphoreType.DMA((len(small),)),
            pltpu.SemaphoreType.DMA,
            pltpu.SemaphoreType.DMA((8,)),
            pltpu.SemaphoreType.DMA((6,)),
            pltpu.SemaphoreType.DMA((6,)),
        ]
        + [pltpu.SemaphoreType.DMA((1 + len(GROUPS) + 2 * len(NEAR),))] * 2,
        compiler_params=pltpu.CompilerParams(collective_id=0, has_side_effects=True, vmem_limit_bytes=VMEM_BYTES),
        name="main",
    )(*(pltpu.with_memory_space_constraint(a, pltpu.HBM) for a in (cells,) + small))
    chunks = ROWS * COLS // CHUNK
    out = pl.pallas_call(
        last_kernel,
        out_shape=shape(ROWS * COLS, N),
        in_specs=[VM, VM, VM, HBM],
        out_specs=HBM,
        scratch_shapes=[
            pltpu.VMEM((ROWS * COLS, N), F32),
            pltpu.VMEM((ROWS * COLS, N), F32),
            pltpu.SemaphoreType.DMA,
            pltpu.SemaphoreType.DMA((chunks,)),
        ],
        compiler_params=pltpu.CompilerParams(vmem_limit_bytes=VMEM_BYTES),
        name="last",
    )(gram, proj, tt, pltpu.with_memory_space_constraint(ensemble.reshape(ROWS * COLS, N), pltpu.HBM))
    return out.reshape(ROWS, COLS, N)


def solution(mesh):
    placed = (
        P("lat", "lon", None),
        P(None, "lat", "lon", None),
        P(None, "lat", "lon", None),
        P(None, "lat", "lon", None, None),
        P(None, "lat", "lon", None, None),
        P(None, "lat", "lon", None),
        P(None, "lat", "lon", None, None),
    )
    return jax.shard_map(
        local, mesh=mesh, in_specs=placed, out_specs=P("lat", "lon", None), check_vma=False
    )
```

```python
import functools
import math
import jax
import jax.numpy as jnp
from jax import lax
from jax.experimental import pallas as pl
from jax.experimental.pallas import tpu as pltpu
from jax.sharding import PartitionSpec as P

MESH = pl.DeviceIdType.MESH
F32 = jnp.float32
BF16 = jnp.bfloat16
ROWS, COLS, N = 32, 128, 128
SLOTS = 8
LATS, LONS = 24, 32
YS, XS = 8, 4
AROUND = ((-1, -1), (-1, 0), (-1, 1), (0, -1), (0, 1), (1, -1), (1, 0), (1, 1))
THIRDS = ((0, 3, -1), (3, 5, 0), (5, 8, 1))
NB = N // 8
NEAR = (-2, -1, 1, 2)
OWN = len(NEAR)
SLOT = sorted(
    ((dx, dy) for dx in (-1, 0, 1, 2) for dy in (-3, -2, -1, 0, 1, 2, 3, 4)), key=lambda p: (abs(p[0]) + abs(p[1]), p)
)
HOPS = [abs(dx) + abs(dy) for dx, dy in SLOT]
CUTS = (0, sum(h <= 2 for h in HOPS), sum(h <= 3 for h in HOPS), sum(h <= 4 for h in HOPS), LONS)
GROUPS = tuple(zip(CUTS[:-1], CUTS[1:]))
PAIRS = SLOTS // 2 + 1
VMEM_BYTES = 48 * 2**20


def split3(x):
    high = x.astype(BF16).astype(F32)
    rest = x - high
    mid = rest.astype(BF16).astype(F32)
    return high, mid, rest - mid


def outer8(r, g):
    rh, rm, rl = split3(r)
    gh, gm, gl = split3(g)
    lhs = jnp.concatenate([rh, rh, rm, rh, rl, rm], axis=0).astype(BF16)
    rhs = jnp.concatenate([gh, gm, gh, gl, gh, gm], axis=0).astype(BF16)
    return lax.dot_general(lhs, rhs, (((0,), (0,)), ((), ())), preferred_element_type=F32)


def spread_row(x, k):
    return jnp.broadcast_to(x[k : k + 1, :], (8, N))


def spread_col(x, c):
    return jnp.broadcast_to(x[:, c : c + 1], (8, N))


def transform_t(gram, proj):
    lane = lax.broadcasted_iota(jnp.int32, (8, N), 1)
    sub = lax.broadcasted_iota(jnp.int32, (8, N), 0)
    prow = jnp.broadcast_to(proj, (8, N))
    w = [gram[8 * i : 8 * i + 8, :] + jnp.where(lane == sub + 8 * i, N - 1.0, 0.0) for i in range(NB)]
    inverse, sums = [], []
    acc = jnp.zeros((8, N), F32)
    for j in range(NB):
        c0 = 8 * j
        wj = w[j]
        cols = [spread_col(wj, c0 + k) for k in range(8)]
        here = (lane >= c0) & (lane < c0 + 8)
        f = jnp.where(here, jnp.where(lane == sub + c0, 1.0, 0.0), wj)
        for k in range(8):
            d = spread_row(cols[k], k)
            below = jnp.where(sub == k, 0.0, cols[k])
            inv = 1.0 / d
            if k:
                lower = jnp.where(sub == k, f, lower)
                diag = jnp.where(sub == k, d, diag)
                inverse_diag = jnp.where(sub == k, inv, inverse_diag)
            else:
                lower, diag, inverse_diag = f, d, inv
            for t in range(k + 1, 8):
                cols[t] = cols[t] - (below * spread_row(cols[t], k)) * inv
            f = f - (below * spread_row(f, k)) * inv
        g = f * inverse_diag
        lj = jnp.where(lane <= c0 + 7, lower * lax.rsqrt(diag), 0.0)
        inverse.append(lj)
        sums.append(jnp.sum(lj, axis=1, keepdims=True))
        acc = acc + lj * jnp.sum(lj * prow, axis=1, keepdims=True)
        if j < NB - 1:
            nxt = w[j + 1]
            terms = [spread_col(nxt, c0 + k) * spread_row(g, k) for k in range(8)]
            while len(terms) > 1:
                terms = [a + b for a, b in zip(terms[::2], terms[1::2])]
            upd = jnp.where(here, 0.0, nxt) - terms[0]
            if j < NB - 2:
                p = outer8(wj, g)
                for i in range(j + 2, NB):
                    w[i] = jnp.where(here, 0.0, w[i]) - p[8 * i : 8 * i + 8, :]
            w[j + 1] = upd
    weights = jnp.sum(acc, axis=0, keepdims=True)
    total = jnp.sum(weights, axis=1, keepdims=True)
    root = math.sqrt(N - 1.0)
    out = []
    for i in range(NB):
        fix = (1.0 - (root * sums[i] + total)) * (1.0 / N)
        out.append(root * inverse[i] + weights + fix)
    return jnp.concatenate(out, axis=0)


def times(x, tt):
    return lax.dot_general(
        x, tt, (((1,), (1,)), ((), ())), precision=lax.Precision.HIGHEST, preferred_element_type=F32
    )


def position():
    lat, lon = lax.axis_index("lat"), lax.axis_index("lon")
    return lat, lon, lon // YS, lax.rem(lon, YS)


def inside(lat, step):
    return (lat + step >= 0) & (lat + step < LATS)


def east_west(lon):
    return lax.rem(lon + 1, LONS), lax.rem(lon + LONS - 1, LONS)


def lon_at(x, y, dx, dy):
    return lax.rem(x + dx + XS, XS) * YS + lax.rem(y + dy + YS, YS)


def announce(pos):
    lat, lon, x, y = pos
    barrier = pltpu.get_barrier_semaphore()

    def greet(a, c):
        pl.semaphore_signal(barrier, inc=1, device_id=(a, c), device_id_type=MESH)

    east, west = east_west(lon)
    for step in NEAR:

        @pl.when(inside(lat, step))
        def _():
            greet(lat + step, lon)
            if abs(step) == 1:
                greet(lat + step, east)
                greet(lat + step, west)

    greet(lat, east)
    greet(lat, west)
    for t in range(1, YS):
        greet(lat, lon_at(x, y, 0, t))
    for t in range(1, XS):
        greet(lat, lon_at(x, y, t, 0))


def enter(pos):
    lat = pos[0]
    count = YS - 1 + XS - 1 + 2
    for step in NEAR:
        count = count + jnp.where(inside(lat, step), 3 if abs(step) == 1 else 1, 0)
    pl.semaphore_wait(pltpu.get_barrier_semaphore(), count)


def pass_on(pos, ready):
    lat, _, x, y = pos
    for t in range(1, YS):
        pl.semaphore_signal(ready, inc=1, device_id=(lat, lon_at(x, y, 0, t)), device_id_type=MESH)


def masks(pos, batch, pattern_ref, mark, markv, pick):
    lat, lon, x, y = pos

    @pl.loop(0, OWN + 1)
    def _(d):
        line = jnp.where(d == OWN, 2, jnp.where(d < 2, d, d + 1))
        for i, (dx, dy) in enumerate(SLOT):
            value = pattern_ref[batch, line, 0, lon_at(x, y, dx, dy)].astype(F32)
            both = jnp.full((PAIRS - 1, 2, N), value, F32).astype(BF16)
            mark[d, i, pl.ds(0, PAIRS - 1)] = both
            mark[d, i, PAIRS - 1] = jnp.zeros((2, N), BF16)
            markv[d, i, pl.ds(0, PAIRS - 1)] = jnp.zeros((PAIRS - 1, 2, N), BF16)
            markv[d, i, PAIRS - 1] = both[0]

    first = (lax.broadcasted_iota(jnp.int32, (16, N), 1) == 0).astype(F32).astype(BF16)
    for d in range(OWN + 1):
        pick[d] = lax.dot_general(
            first, markv[d].reshape(LONS * PAIRS * 2, N), (((1,), (1,)), ((), ())), preferred_element_type=F32
        ).astype(BF16)


def observe(batch, prior, observed_ref, precision_ref, owned_ref):
    sub = lax.broadcasted_iota(jnp.int32, (SLOTS, N), 0)
    obs = jnp.zeros((SLOTS, N), F32)
    prec = jnp.zeros((SLOTS, N), F32)
    own = jnp.zeros((SLOTS, N), F32)
    for o in range(SLOTS):
        obs = jnp.where(sub == o, observed_ref[batch, 0, o], obs)
        prec = jnp.where(sub == o, precision_ref[batch, 0, o], prec)
        own = jnp.where(sub == o, owned_ref[batch, 0, o].astype(F32), own)
    root = jnp.sqrt(prec) * own
    mean = jnp.sum(prior, axis=1, keepdims=True) * (1.0 / N)
    scaled = (root * (prior - mean)).astype(BF16)
    innov = (root * (obs - mean)).astype(BF16)
    vector = jnp.sum(scaled.astype(F32) * innov.astype(F32), axis=0, keepdims=True)
    return scaled, vector


class Exchange:
    def __init__(self, pos, seen, sems):
        self.pos, self.seen, self.sems = pos, seen, sems

    def copy(self, src, size, dst, device, send, recv):
        (sd, si), (dd, di) = src, dst
        return pltpu.make_async_remote_copy(
            src_ref=self.seen.at[sd, pl.ds(si, size)], dst_ref=self.seen.at[dd, pl.ds(di, size)],
            send_sem=self.sems.at[send], recv_sem=self.sems.at[recv], device_id=device, device_id_type=MESH,
        )

    def blank(self):
        for step in NEAR:

            @pl.when(jnp.logical_not(inside(self.pos[0], step)))
            def _():
                self.seen[NEAR.index(step)] = jnp.zeros(self.seen.shape[1:], BF16)

    def row(self, i, g):
        lat, _, x, y = self.pos
        dx, dy = SLOT[i]
        return self.copy((OWN, 0), 1, (OWN, i), (lat, lon_at(x, y, -dx, -dy)), 0, 1 + g)

    def row_group(self, g):
        start, stop = max(GROUPS[g][0], 1), GROUPS[g][1]
        return self.copy((OWN, start), stop - start, (OWN, start), self.pos[:2], 0, 1 + g)

    def relay(self, k, start, stop):
        lat, lon = self.pos[:2]
        send = 1 + len(GROUPS) + k
        return self.copy(
            (OWN, start), stop - start, (OWN - 1 - k, start), (lat + NEAR[k], lon), send, send + len(NEAR)
        )

    def start(self, scaled, vector):
        for i in range(PAIRS - 1):
            self.seen[OWN, 0, i] = scaled[2 * i : 2 * i + 2, :]
        high = vector.astype(BF16)
        self.seen[OWN, 0, PAIRS - 1] = jnp.concatenate([high.astype(F32), vector - high.astype(F32)], axis=0).astype(BF16)
        for g, (start, stop) in reversed(tuple(enumerate(GROUPS))):
            for i in reversed(range(max(start, 1), stop)):
                self.row(i, g).start()

    def finish(self, mark, pick):
        lat = self.pos[0]

        def term(d, size):
            flat = self.seen[pl.ds(d, size)].reshape(size * LONS * PAIRS * 2, N)
            marked = flat * mark[pl.ds(d, size)].reshape(size * LONS * PAIRS * 2, N)
            gram = lax.dot_general(marked, flat, (((0,), (0,)), ((), ())), preferred_element_type=F32)
            proj = jnp.zeros((16, N), F32)
            for i in range(size):
                rows = flat[i * LONS * PAIRS * 2 : (i + 1) * LONS * PAIRS * 2]
                proj = proj + jnp.dot(pick[d + i], rows, preferred_element_type=F32)
            return gram, proj[0:1]

        for g, (start, stop) in enumerate(GROUPS):
            self.row_group(g).wait_recv()
            for k, step in enumerate(NEAR):

                @pl.when(inside(lat, step))
                def _():
                    self.relay(k, start, stop).start()

        gram, proj = term(OWN, 1)
        for k, step in enumerate(NEAR):

            @pl.when(inside(lat, -step))
            def _():
                self.relay(k, 0, LONS).wait_recv()

        more, morev = term(0, OWN)
        return gram + more, proj + morev

    def drain(self):
        self.copy((OWN, 1), LONS - 1, (OWN, 1), self.pos[:2], 0, 1).wait_send()
        for k, step in enumerate(NEAR):

            @pl.when(inside(self.pos[0], step))
            def _():
                self.relay(k, 0, LONS).wait_send()


class Around:
    def __init__(self, pos, src, dst, sems):
        self.pos, self.src, self.dst, self.sems = pos, src, dst, sems

    def copies(self, g):
        lat, lon = self.pos[:2]
        start, stop, step = THIRDS[g]
        return [
            pltpu.make_async_remote_copy(
                src_ref=self.src.at[n], dst_ref=self.dst.at[7 - n],
                send_sem=self.sems.at[g], recv_sem=self.sems.at[5 - g],
                device_id=(lat + step, lax.rem(lon + AROUND[n][1] + LONS, LONS)), device_id_type=MESH,
            )
            for n in range(start, stop)
        ]

    def group(self, g):
        start, stop, _ = THIRDS[g]
        return pltpu.make_async_remote_copy(
            src_ref=self.src.at[pl.ds(start, stop - start)], dst_ref=self.dst.at[pl.ds(start, stop - start)],
            send_sem=self.sems.at[g], recv_sem=self.sems.at[3 + g], device_id=self.pos[:2], device_id_type=MESH,
        )

    def each(self, act):
        for g, (_, _, step) in enumerate(THIRDS):
            if step == 0:
                act(g)
            else:
                pl.when(inside(self.pos[0], step))(functools.partial(act, g))

    def blank(self):
        for start, stop, step in THIRDS:

            @pl.when(jnp.logical_not(inside(self.pos[0], step)))
            def _():
                self.dst[pl.ds(start, stop - start)] = jnp.zeros((stop - start, SLOTS, N), F32)

    def start(self):
        def act(g):
            for c in self.copies(g):
                c.start()

        self.each(act)

    def arrive(self):
        self.each(lambda g: self.group(g).wait_recv())

    def drain(self):
        self.each(lambda g: self.group(g).wait_send())


class Halo:
    def __init__(self, pos, sems, rows, ends, sides, targets):
        self.pos, self.sems, self.rows, self.ends, self.sides, self.targets = pos, sems, rows, ends, sides, targets

    def copy(self, src, dst, recv, device):
        return pltpu.make_async_remote_copy(
            src_ref=src, dst_ref=dst, send_sem=self.sems.at[recv], recv_sem=self.sems.at[4 + recv],
            device_id=device, device_id_type=MESH,
        )

    def across(self):
        lat, lon = self.pos[:2]
        east, west = east_west(lon)
        left, right = self.targets["sides"]
        return [self.copy(self.sides[1], left, 0, (lat, east)), self.copy(self.sides[0], right, 1, (lat, west))]

    def along(self, step):
        lat, lon = self.pos[:2]
        east, west = east_west(lon)
        which, to = (1, 0) if step == 1 else (0, 1)
        row, first, last, _ = self.targets["rows"][to]
        return [
            self.copy(self.ends[which][1], first, 2 + to, (lat + step, east)),
            self.copy(self.ends[which][0], last, 2 + to, (lat + step, west)),
            self.copy(self.rows[which], row, 2 + to, (lat + step, lon)),
        ]

    def whole(self, step):
        to = 0 if step == 1 else 1
        row = self.targets["rows"][to][3]
        return self.copy(row, row, 2 + to, self.pos[:2])

    def start(self):
        for step in (1, -1):

            @pl.when(inside(self.pos[0], step))
            def _():
                for c in self.along(step):
                    c.start()

        for c in self.across():
            c.start()

    def arrive(self):
        for c in self.across():
            c.wait_recv()
        for step in (1, -1):

            @pl.when(inside(self.pos[0], -step))
            def _():
                self.whole(step).wait_recv()

    def drain(self):
        for c in self.across():
            c.wait_send()
        for step in (1, -1):

            @pl.when(inside(self.pos[0], step))
            def _():
                self.whole(step).wait_send()


def corner(stencil_ref, batch, o):
    s = stencil_ref[batch, 0, o]
    r = s // (COLS + 2)
    return r, s - r * (COLS + 2)


def main_kernel(
    cells, observed_in, precision_in, weight_in, stencil_in, owned_in, pattern_in,
    gram_ref, proj_ref, tt_ref,
    observed, precision, weight, stencil, owned, pattern,
    tile, prior, ask, asked, answer, answered, seen0, seen1, mark, markv, pick,
    small_sem, inner_sem, ready, halo_sem, ask_sem, answer_sem, sem0, sem1,
):
    pos = position()
    lat = pos[0]
    announce(pos)
    inner = pltpu.make_async_copy(cells, tile.at[pl.ds(1, ROWS), pl.ds(1, COLS)], inner_sem)
    inner.start()
    smalls = [
        pltpu.make_async_copy(src, dst, small_sem.at[i])
        for i, (src, dst) in enumerate(
            (
                (pattern_in, pattern),
                (observed_in, observed),
                (precision_in, precision),
                (weight_in, weight),
                (stencil_in, stencil),
                (owned_in, owned),
            )
        )
    ]
    for c in smalls:
        c.start()
    first = Exchange(pos, seen0, sem0)
    second = Exchange(pos, seen1, sem1)
    asks = Around(pos, ask.at[pl.ds(0, 8)], asked, ask_sem)
    answers = Around(pos, answer, answered, answer_sem)
    for part in (first, second, asks, answers):
        part.blank()
    for step, r in ((-1, 0), (1, ROWS + 1)):

        @pl.when(jnp.logical_not(inside(lat, step)))
        def _():
            tile[r] = jnp.zeros((COLS + 2, 1, N), F32)

    halo = Halo(
        pos,
        halo_sem,
        rows=(tile.at[1, pl.ds(1, COLS)], tile.at[ROWS, pl.ds(1, COLS)]),
        ends=((tile.at[1, 1], tile.at[1, COLS]), (tile.at[ROWS, 1], tile.at[ROWS, COLS])),
        sides=(tile.at[pl.ds(1, ROWS), 1], tile.at[pl.ds(1, ROWS), COLS]),
        targets={
            "sides": (tile.at[pl.ds(1, ROWS), 0], tile.at[pl.ds(1, ROWS), COLS + 1]),
            "rows": tuple(
                (tile.at[r, pl.ds(1, COLS)], tile.at[r, 0], tile.at[r, COLS + 1], tile.at[r]) for r in (0, ROWS + 1)
            ),
        },
    )
    inner.wait()
    enter(pos)
    halo.start()
    pass_on(pos, ready)
    for c in smalls:
        c.wait()
    masks(pos, 0, pattern, mark.at[0], markv, pick.at[0])
    halo.arrive()

    for o in range(SLOTS):
        r, c = corner(stencil, 0, o)
        total = jnp.zeros((1, N), F32)
        for k in range(4):
            total = total + weight[0, k, o] * tile[r + k // 2, c + k % 2]
        prior[pl.ds(o, 1), :] = total
    scaled, vector = observe(0, prior[...], observed, precision, owned)
    pl.semaphore_wait(ready, YS - 1)
    first.start(scaled, vector)

    for o in range(SLOTS):
        r, c = corner(stencil, 1, o)
        shares = [jnp.zeros((1, N), F32) for _ in range(9)]
        for k in range(4):
            rk, ck = r + k // 2, c + k % 2
            up, down = rk == 0, rk == ROWS + 1
            left, right = ck == 0, ck == COLS + 1
            middle, centre = jnp.logical_not(up | down), jnp.logical_not(left | right)
            cell, scale = tile[rk, ck], weight[1, k, o]
            for n, (dr, dc) in enumerate(AROUND + ((0, 0),)):
                there = (up, middle, down)[dr + 1] & (left, centre, right)[dc + 1]
                shares[n] = shares[n] + jnp.where(there, scale, 0.0) * cell
        for n in range(9):
            ask[n, pl.ds(o, 1), :] = shares[n]
    asks.start()
    masks(pos, 1, pattern, mark.at[1], markv, pick.at[1])
    gram, proj = first.finish(mark.at[0], pick.at[0])
    asks.arrive()

    tt = transform_t(gram, proj)
    answer[...] = times(asked[...].reshape(8 * SLOTS, N), tt).reshape(8, SLOTS, N)
    answers.start()
    tt_ref[...] = tt
    total = times(ask[8], tt)
    for part in (halo, first, asks):
        part.drain()
    answers.arrive()
    for n in range(8):
        total = total + answered[n]
    second.start(*observe(1, total, observed, precision, owned))
    gram_ref[...], proj_ref[...] = second.finish(mark.at[1], pick.at[1])
    for part in (answers, second):
        part.drain()


CHUNK = 1024


def last_kernel(gram, proj, tt_ref, ens, out, cells, moved, in_sem, out_sem):
    chunks = ROWS * COLS // CHUNK
    load = pltpu.make_async_copy(ens, cells, in_sem)
    load.start()
    tt = transform_t(gram[...], proj[...])
    both = jnp.dot(tt, tt_ref[...], precision=lax.Precision.HIGHEST, preferred_element_type=F32)
    high = both.astype(BF16)
    low = (both - high.astype(F32)).astype(BF16)
    right = jnp.concatenate(
        [jnp.concatenate([high, high], axis=1), jnp.concatenate([low, jnp.zeros_like(low)], axis=1)], axis=0
    )
    stores = []
    load.wait()
    for i in range(chunks):
        rows = pl.ds(i * CHUNK, CHUNK)
        xs = cells[rows, :]
        xh = xs.astype(BF16)
        xl = (xs - xh.astype(F32)).astype(BF16)
        res = lax.dot_general(
            jnp.concatenate([xh, xl], axis=1), right, (((1,), (1,)), ((), ())), preferred_element_type=F32
        )
        moved[rows, :] = res[:, :N] + res[:, N:]
        c = pltpu.make_async_copy(moved.at[rows], out.at[rows], out_sem.at[i])
        c.start()
        stores.append(c)
    for c in stores:
        c.wait()


def shape(*dims):
    return jax.ShapeDtypeStruct(dims, F32)


VM = pl.BlockSpec(memory_space=pltpu.VMEM)
HBM = pl.BlockSpec(memory_space=pltpu.HBM)


def local(ensemble, observed, precision, interp_weight, stencil, owned, pattern):
    cells = ensemble.reshape(ROWS, COLS, 1, N)
    small = (
        observed.reshape(2, 1, SLOTS),
        precision.reshape(2, 1, SLOTS),
        interp_weight.reshape(2, 4, SLOTS),
        stencil.reshape(2, 4, SLOTS),
        owned.reshape(2, 1, SLOTS),
        pattern.transpose(0, 1, 3, 2, 4).reshape(2, 5, 1, LONS),
    )
    gram, proj, tt = pl.pallas_call(
        main_kernel,
        out_shape=(shape(N, N), shape(1, N), shape(N, N)),
        in_specs=[HBM] * 7,
        out_specs=(VM, VM, VM),
        scratch_shapes=[pltpu.SMEM(a.shape, a.dtype) for a in small]
        + [
            pltpu.VMEM((ROWS + 2, COLS + 2, 1, N), F32),
            pltpu.VMEM((SLOTS, N), F32),
            pltpu.VMEM((9, SLOTS, N), F32),
            pltpu.VMEM((8, SLOTS, N), F32),
            pltpu.VMEM((8, SLOTS, N), F32),
            pltpu.VMEM((8, SLOTS, N), F32),
            pltpu.VMEM((5, LONS, PAIRS, 2, N), BF16),
            pltpu.VMEM((5, LONS, PAIRS, 2, N), BF16),
            pltpu.VMEM((2, 5, LONS, PAIRS, 2, N), BF16),
            pltpu.VMEM((5, LONS, PAIRS, 2, N), BF16),
            pltpu.VMEM((2, 5, 16, LONS * PAIRS * 2), BF16),
            pltpu.SemaphoreType.DMA((len(small),)),
            pltpu.SemaphoreType.DMA,
            pltpu.SemaphoreType.REGULAR,
            pltpu.SemaphoreType.DMA((8,)),
            pltpu.SemaphoreType.DMA((6,)),
            pltpu.SemaphoreType.DMA((6,)),
        ]
        + [pltpu.SemaphoreType.DMA((1 + len(GROUPS) + 2 * len(NEAR),))] * 2,
        compiler_params=pltpu.CompilerParams(collective_id=0, has_side_effects=True, vmem_limit_bytes=VMEM_BYTES),
        name="main",
    )(*(pltpu.with_memory_space_constraint(a, pltpu.HBM) for a in (cells,) + small))
    chunks = ROWS * COLS // CHUNK
    out = pl.pallas_call(
        last_kernel,
        out_shape=shape(ROWS * COLS, N),
        in_specs=[VM, VM, VM, HBM],
        out_specs=HBM,
        scratch_shapes=[
            pltpu.VMEM((ROWS * COLS, N), F32),
            pltpu.VMEM((ROWS * COLS, N), F32),
            pltpu.SemaphoreType.DMA,
            pltpu.SemaphoreType.DMA((chunks,)),
        ],
        compiler_params=pltpu.CompilerParams(vmem_limit_bytes=VMEM_BYTES),
        name="last",
    )(gram, proj, tt, pltpu.with_memory_space_constraint(ensemble.reshape(ROWS * COLS, N), pltpu.HBM))
    return out.reshape(ROWS, COLS, N)


def solution(mesh):
    placed = (
        P("lat", "lon", None),
        P(None, "lat", "lon", None),
        P(None, "lat", "lon", None),
        P(None, "lat", "lon", None, None),
        P(None, "lat", "lon", None, None),
        P(None, "lat", "lon", None),
        P(None, "lat", "lon", None, None),
    )
    return jax.shard_map(
        local, mesh=mesh, in_specs=placed, out_specs=P("lat", "lon", None), check_vma=False
    )
```

```python
import functools
import math
import jax
import jax.numpy as jnp
from jax import lax
from jax.experimental import pallas as pl
from jax.experimental.pallas import tpu as pltpu
from jax.sharding import PartitionSpec as P

MESH = pl.DeviceIdType.MESH
F32 = jnp.float32
BF16 = jnp.bfloat16
ROWS, COLS, N = 32, 128, 128
SLOTS = 8
LATS, LONS = 24, 32
YS, XS = 8, 4
AROUND = ((-1, -1), (-1, 0), (-1, 1), (0, -1), (0, 1), (1, -1), (1, 0), (1, 1))
THIRDS = ((0, 3, -1), (3, 5, 0), (5, 8, 1))
DEEP = 16
NB = N // DEEP
NEAR = (-2, -1, 1, 2)
OWN = len(NEAR)
SLOT = sorted(
    ((dx, dy) for dx in (-1, 0, 1, 2) for dy in (-3, -2, -1, 0, 1, 2, 3, 4)), key=lambda p: (abs(p[0]) + abs(p[1]), p)
)
HOPS = [abs(dx) + abs(dy) for dx, dy in SLOT]
CUTS = (0, sum(h <= 2 for h in HOPS), sum(h <= 3 for h in HOPS), sum(h <= 4 for h in HOPS), LONS)
GROUPS = tuple(zip(CUTS[:-1], CUTS[1:]))
PAIRS = SLOTS // 2 + 1
VMEM_BYTES = 48 * 2**20


def split3(x):
    high = x.astype(BF16).astype(F32)
    rest = x - high
    mid = rest.astype(BF16).astype(F32)
    return high, mid, rest - mid


def outer(r, g):
    rh, rm, rl = split3(r)
    gh, gm, gl = split3(g)
    lhs = jnp.concatenate([rh, rh, rm, rh, rl, rm], axis=0).astype(BF16)
    rhs = jnp.concatenate([gh, gm, gh, gl, gh, gm], axis=0).astype(BF16)
    return lax.dot_general(lhs, rhs, (((0,), (0,)), ((), ())), preferred_element_type=F32)


def spread_row(x, k):
    return jnp.broadcast_to(x[k : k + 1, :], (DEEP, N))


def spread_col(x, c):
    return jnp.broadcast_to(x[:, c : c + 1], (DEEP, N))


def transform_t(gram, proj):
    lane = lax.broadcasted_iota(jnp.int32, (DEEP, N), 1)
    sub = lax.broadcasted_iota(jnp.int32, (DEEP, N), 0)
    prow = jnp.broadcast_to(proj, (DEEP, N))
    w = [gram[DEEP * i : DEEP * i + DEEP, :] + jnp.where(lane == sub + DEEP * i, N - 1.0, 0.0) for i in range(NB)]
    inverse, sums = [], []
    acc = jnp.zeros((DEEP, N), F32)
    for j in range(NB):
        c0 = DEEP * j
        wj = w[j]
        cols = [spread_col(wj, c0 + k) for k in range(DEEP)]
        here = (lane >= c0) & (lane < c0 + DEEP)
        f = jnp.where(here, jnp.where(lane == sub + c0, 1.0, 0.0), wj)
        for k in range(DEEP):
            d = spread_row(cols[k], k)
            below = jnp.where(sub == k, 0.0, cols[k])
            inv = 1.0 / d
            if k:
                lower = jnp.where(sub == k, f, lower)
                diag = jnp.where(sub == k, d, diag)
                inverse_diag = jnp.where(sub == k, inv, inverse_diag)
            else:
                lower, diag, inverse_diag = f, d, inv
            for t in range(k + 1, DEEP):
                cols[t] = cols[t] - (below * spread_row(cols[t], k)) * inv
            f = f - (below * spread_row(f, k)) * inv
        g = f * inverse_diag
        lj = jnp.where(lane <= c0 + DEEP - 1, lower * lax.rsqrt(diag), 0.0)
        inverse.append(lj)
        sums.append(jnp.sum(lj, axis=1, keepdims=True))
        acc = acc + lj * jnp.sum(lj * prow, axis=1, keepdims=True)
        if j < NB - 1:
            nxt = w[j + 1]
            terms = [spread_col(nxt, c0 + k) * spread_row(g, k) for k in range(DEEP)]
            while len(terms) > 1:
                terms = [a + b for a, b in zip(terms[::2], terms[1::2])]
            upd = jnp.where(here, 0.0, nxt) - terms[0]
            if j < NB - 2:
                p = outer(wj, g)
                for i in range(j + 2, NB):
                    w[i] = jnp.where(here, 0.0, w[i]) - p[DEEP * i : DEEP * i + DEEP, :]
            w[j + 1] = upd
    weights = jnp.sum(acc, axis=0, keepdims=True)
    total = jnp.sum(weights, axis=1, keepdims=True)
    root = math.sqrt(N - 1.0)
    out = []
    for i in range(NB):
        fix = (1.0 - (root * sums[i] + total)) * (1.0 / N)
        out.append(root * inverse[i] + weights + fix)
    return jnp.concatenate(out, axis=0)


def times(x, tt):
    return lax.dot_general(
        x, tt, (((1,), (1,)), ((), ())), precision=lax.Precision.HIGHEST, preferred_element_type=F32
    )


def position():
    lat, lon = lax.axis_index("lat"), lax.axis_index("lon")
    return lat, lon, lon // YS, lax.rem(lon, YS)


def inside(lat, step):
    return (lat + step >= 0) & (lat + step < LATS)


def east_west(lon):
    return lax.rem(lon + 1, LONS), lax.rem(lon + LONS - 1, LONS)


def lon_at(x, y, dx, dy):
    return lax.rem(x + dx + XS, XS) * YS + lax.rem(y + dy + YS, YS)


def announce(pos):
    lat, lon, x, y = pos
    barrier = pltpu.get_barrier_semaphore()

    def greet(a, c):
        pl.semaphore_signal(barrier, inc=1, device_id=(a, c), device_id_type=MESH)

    east, west = east_west(lon)
    for step in NEAR:

        @pl.when(inside(lat, step))
        def _():
            greet(lat + step, lon)
            if abs(step) == 1:
                greet(lat + step, east)
                greet(lat + step, west)

    greet(lat, east)
    greet(lat, west)
    for t in range(1, YS):
        greet(lat, lon_at(x, y, 0, t))
    for t in range(1, XS):
        greet(lat, lon_at(x, y, t, 0))


def enter(pos):
    lat = pos[0]
    count = YS - 1 + XS - 1 + 2
    for step in NEAR:
        count = count + jnp.where(inside(lat, step), 3 if abs(step) == 1 else 1, 0)
    pl.semaphore_wait(pltpu.get_barrier_semaphore(), count)


def pass_on(pos, ready):
    lat, _, x, y = pos
    for t in range(1, YS):
        pl.semaphore_signal(ready, inc=1, device_id=(lat, lon_at(x, y, 0, t)), device_id_type=MESH)


def masks(pos, batch, pattern_ref, mark, markv, pick):
    lat, lon, x, y = pos

    @pl.loop(0, OWN + 1)
    def _(d):
        line = jnp.where(d == OWN, 2, jnp.where(d < 2, d, d + 1))
        for i, (dx, dy) in enumerate(SLOT):
            value = pattern_ref[batch, line, 0, lon_at(x, y, dx, dy)].astype(F32)
            both = jnp.full((PAIRS - 1, 2, N), value, F32).astype(BF16)
            mark[d, i, pl.ds(0, PAIRS - 1)] = both
            mark[d, i, PAIRS - 1] = jnp.zeros((2, N), BF16)
            markv[d, i, pl.ds(0, PAIRS - 1)] = jnp.zeros((PAIRS - 1, 2, N), BF16)
            markv[d, i, PAIRS - 1] = both[0]

    first = (lax.broadcasted_iota(jnp.int32, (16, N), 1) == 0).astype(F32).astype(BF16)
    for d in range(OWN + 1):
        pick[d] = lax.dot_general(
            first, markv[d].reshape(LONS * PAIRS * 2, N), (((1,), (1,)), ((), ())), preferred_element_type=F32
        ).astype(BF16)


def observe(batch, prior, observed_ref, precision_ref, owned_ref):
    sub = lax.broadcasted_iota(jnp.int32, (SLOTS, N), 0)
    obs = jnp.zeros((SLOTS, N), F32)
    prec = jnp.zeros((SLOTS, N), F32)
    own = jnp.zeros((SLOTS, N), F32)
    for o in range(SLOTS):
        obs = jnp.where(sub == o, observed_ref[batch, 0, o], obs)
        prec = jnp.where(sub == o, precision_ref[batch, 0, o], prec)
        own = jnp.where(sub == o, owned_ref[batch, 0, o].astype(F32), own)
    root = jnp.sqrt(prec) * own
    mean = jnp.sum(prior, axis=1, keepdims=True) * (1.0 / N)
    scaled = (root * (prior - mean)).astype(BF16)
    innov = (root * (obs - mean)).astype(BF16)
    vector = jnp.sum(scaled.astype(F32) * innov.astype(F32), axis=0, keepdims=True)
    return scaled, vector


class Exchange:
    def __init__(self, pos, seen, sems):
        self.pos, self.seen, self.sems = pos, seen, sems

    def copy(self, src, size, dst, device, send, recv):
        (sd, si), (dd, di) = src, dst
        return pltpu.make_async_remote_copy(
            src_ref=self.seen.at[sd, pl.ds(si, size)], dst_ref=self.seen.at[dd, pl.ds(di, size)],
            send_sem=self.sems.at[send], recv_sem=self.sems.at[recv], device_id=device, device_id_type=MESH,
        )

    def blank(self):
        for step in NEAR:

            @pl.when(jnp.logical_not(inside(self.pos[0], step)))
            def _():
                self.seen[NEAR.index(step)] = jnp.zeros(self.seen.shape[1:], BF16)

    def row(self, i, g):
        lat, _, x, y = self.pos
        dx, dy = SLOT[i]
        return self.copy((OWN, 0), 1, (OWN, i), (lat, lon_at(x, y, -dx, -dy)), 0, 1 + g)

    def row_group(self, g):
        start, stop = max(GROUPS[g][0], 1), GROUPS[g][1]
        return self.copy((OWN, start), stop - start, (OWN, start), self.pos[:2], 0, 1 + g)

    def relay(self, k, start, stop):
        lat, lon = self.pos[:2]
        send = 1 + len(GROUPS) + k
        return self.copy(
            (OWN, start), stop - start, (OWN - 1 - k, start), (lat + NEAR[k], lon), send, send + len(NEAR)
        )

    def start(self, scaled, vector):
        for i in range(PAIRS - 1):
            self.seen[OWN, 0, i] = scaled[2 * i : 2 * i + 2, :]
        high = vector.astype(BF16)
        self.seen[OWN, 0, PAIRS - 1] = jnp.concatenate([high.astype(F32), vector - high.astype(F32)], axis=0).astype(BF16)
        for g, (start, stop) in reversed(tuple(enumerate(GROUPS))):
            for i in reversed(range(max(start, 1), stop)):
                self.row(i, g).start()

    def finish(self, mark, pick):
        lat = self.pos[0]

        def term(d, size):
            flat = self.seen[pl.ds(d, size)].reshape(size * LONS * PAIRS * 2, N)
            marked = flat * mark[pl.ds(d, size)].reshape(size * LONS * PAIRS * 2, N)
            gram = lax.dot_general(marked, flat, (((0,), (0,)), ((), ())), preferred_element_type=F32)
            proj = jnp.zeros((16, N), F32)
            for i in range(size):
                rows = flat[i * LONS * PAIRS * 2 : (i + 1) * LONS * PAIRS * 2]
                proj = proj + jnp.dot(pick[d + i], rows, preferred_element_type=F32)
            return gram, proj[0:1]

        for g, (start, stop) in enumerate(GROUPS):
            self.row_group(g).wait_recv()
            for k, step in enumerate(NEAR):

                @pl.when(inside(lat, step))
                def _():
                    self.relay(k, start, stop).start()

        gram, proj = term(OWN, 1)
        for k, step in enumerate(NEAR):

            @pl.when(inside(lat, -step))
            def _():
                self.relay(k, 0, LONS).wait_recv()

        more, morev = term(0, OWN)
        return gram + more, proj + morev

    def drain(self):
        self.copy((OWN, 1), LONS - 1, (OWN, 1), self.pos[:2], 0, 1).wait_send()
        for k, step in enumerate(NEAR):

            @pl.when(inside(self.pos[0], step))
            def _():
                self.relay(k, 0, LONS).wait_send()


class Around:
    def __init__(self, pos, src, dst, sems):
        self.pos, self.src, self.dst, self.sems = pos, src, dst, sems

    def copies(self, g):
        lat, lon = self.pos[:2]
        start, stop, step = THIRDS[g]
        return [
            pltpu.make_async_remote_copy(
                src_ref=self.src.at[n], dst_ref=self.dst.at[7 - n],
                send_sem=self.sems.at[g], recv_sem=self.sems.at[5 - g],
                device_id=(lat + step, lax.rem(lon + AROUND[n][1] + LONS, LONS)), device_id_type=MESH,
            )
            for n in range(start, stop)
        ]

    def group(self, g):
        start, stop, _ = THIRDS[g]
        return pltpu.make_async_remote_copy(
            src_ref=self.src.at[pl.ds(start, stop - start)], dst_ref=self.dst.at[pl.ds(start, stop - start)],
            send_sem=self.sems.at[g], recv_sem=self.sems.at[3 + g], device_id=self.pos[:2], device_id_type=MESH,
        )

    def each(self, act):
        for g, (_, _, step) in enumerate(THIRDS):
            if step == 0:
                act(g)
            else:
                pl.when(inside(self.pos[0], step))(functools.partial(act, g))

    def blank(self):
        for start, stop, step in THIRDS:

            @pl.when(jnp.logical_not(inside(self.pos[0], step)))
            def _():
                self.dst[pl.ds(start, stop - start)] = jnp.zeros((stop - start, SLOTS, N), F32)

    def start(self):
        def act(g):
            for c in self.copies(g):
                c.start()

        self.each(act)

    def arrive(self):
        self.each(lambda g: self.group(g).wait_recv())

    def drain(self):
        self.each(lambda g: self.group(g).wait_send())


class Halo:
    def __init__(self, pos, sems, rows, ends, sides, targets):
        self.pos, self.sems, self.rows, self.ends, self.sides, self.targets = pos, sems, rows, ends, sides, targets

    def copy(self, src, dst, recv, device):
        return pltpu.make_async_remote_copy(
            src_ref=src, dst_ref=dst, send_sem=self.sems.at[recv], recv_sem=self.sems.at[4 + recv],
            device_id=device, device_id_type=MESH,
        )

    def across(self):
        lat, lon = self.pos[:2]
        east, west = east_west(lon)
        left, right = self.targets["sides"]
        return [self.copy(self.sides[1], left, 0, (lat, east)), self.copy(self.sides[0], right, 1, (lat, west))]

    def along(self, step):
        lat, lon = self.pos[:2]
        east, west = east_west(lon)
        which, to = (1, 0) if step == 1 else (0, 1)
        row, first, last, _ = self.targets["rows"][to]
        return [
            self.copy(self.ends[which][1], first, 2 + to, (lat + step, east)),
            self.copy(self.ends[which][0], last, 2 + to, (lat + step, west)),
            self.copy(self.rows[which], row, 2 + to, (lat + step, lon)),
        ]

    def whole(self, step):
        to = 0 if step == 1 else 1
        row = self.targets["rows"][to][3]
        return self.copy(row, row, 2 + to, self.pos[:2])

    def start(self):
        for step in (1, -1):

            @pl.when(inside(self.pos[0], step))
            def _():
                for c in self.along(step):
                    c.start()

        for c in self.across():
            c.start()

    def arrive(self):
        for c in self.across():
            c.wait_recv()
        for step in (1, -1):

            @pl.when(inside(self.pos[0], -step))
            def _():
                self.whole(step).wait_recv()

    def drain(self):
        for c in self.across():
            c.wait_send()
        for step in (1, -1):

            @pl.when(inside(self.pos[0], step))
            def _():
                self.whole(step).wait_send()


def corner(stencil_ref, batch, o):
    s = stencil_ref[batch, 0, o]
    r = s // (COLS + 2)
    return r, s - r * (COLS + 2)


def main_kernel(
    cells, observed_in, precision_in, weight_in, stencil_in, owned_in, pattern_in,
    gram_ref, proj_ref, tt_ref,
    observed, precision, weight, stencil, owned, pattern,
    tile, prior, ask, asked, answer, answered, seen0, seen1, mark, markv, pick,
    small_sem, inner_sem, ready, halo_sem, ask_sem, answer_sem, sem0, sem1,
):
    pos = position()
    lat = pos[0]
    announce(pos)
    inner = pltpu.make_async_copy(cells, tile.at[pl.ds(1, ROWS), pl.ds(1, COLS)], inner_sem)
    inner.start()
    smalls = [
        pltpu.make_async_copy(src, dst, small_sem.at[i])
        for i, (src, dst) in enumerate(
            (
                (pattern_in, pattern),
                (observed_in, observed),
                (precision_in, precision),
                (weight_in, weight),
                (stencil_in, stencil),
                (owned_in, owned),
            )
        )
    ]
    for c in smalls:
        c.start()
    first = Exchange(pos, seen0, sem0)
    second = Exchange(pos, seen1, sem1)
    asks = Around(pos, ask.at[pl.ds(0, 8)], asked, ask_sem)
    answers = Around(pos, answer, answered, answer_sem)
    for part in (first, second, asks, answers):
        part.blank()
    for step, r in ((-1, 0), (1, ROWS + 1)):

        @pl.when(jnp.logical_not(inside(lat, step)))
        def _():
            tile[r] = jnp.zeros((COLS + 2, 1, N), F32)

    halo = Halo(
        pos,
        halo_sem,
        rows=(tile.at[1, pl.ds(1, COLS)], tile.at[ROWS, pl.ds(1, COLS)]),
        ends=((tile.at[1, 1], tile.at[1, COLS]), (tile.at[ROWS, 1], tile.at[ROWS, COLS])),
        sides=(tile.at[pl.ds(1, ROWS), 1], tile.at[pl.ds(1, ROWS), COLS]),
        targets={
            "sides": (tile.at[pl.ds(1, ROWS), 0], tile.at[pl.ds(1, ROWS), COLS + 1]),
            "rows": tuple(
                (tile.at[r, pl.ds(1, COLS)], tile.at[r, 0], tile.at[r, COLS + 1], tile.at[r]) for r in (0, ROWS + 1)
            ),
        },
    )
    inner.wait()
    enter(pos)
    halo.start()
    pass_on(pos, ready)
    for c in smalls:
        c.wait()
    masks(pos, 0, pattern, mark.at[0], markv, pick.at[0])
    halo.arrive()

    for o in range(SLOTS):
        r, c = corner(stencil, 0, o)
        total = jnp.zeros((1, N), F32)
        for k in range(4):
            total = total + weight[0, k, o] * tile[r + k // 2, c + k % 2]
        prior[pl.ds(o, 1), :] = total
    scaled, vector = observe(0, prior[...], observed, precision, owned)
    pl.semaphore_wait(ready, YS - 1)
    first.start(scaled, vector)

    for o in range(SLOTS):
        r, c = corner(stencil, 1, o)
        shares = [jnp.zeros((1, N), F32) for _ in range(9)]
        for k in range(4):
            rk, ck = r + k // 2, c + k % 2
            up, down = rk == 0, rk == ROWS + 1
            left, right = ck == 0, ck == COLS + 1
            middle, centre = jnp.logical_not(up | down), jnp.logical_not(left | right)
            cell, scale = tile[rk, ck], weight[1, k, o]
            for n, (dr, dc) in enumerate(AROUND + ((0, 0),)):
                there = (up, middle, down)[dr + 1] & (left, centre, right)[dc + 1]
                shares[n] = shares[n] + jnp.where(there, scale, 0.0) * cell
        for n in range(9):
            ask[n, pl.ds(o, 1), :] = shares[n]
    asks.start()
    masks(pos, 1, pattern, mark.at[1], markv, pick.at[1])
    gram, proj = first.finish(mark.at[0], pick.at[0])
    asks.arrive()

    tt = transform_t(gram, proj)
    answer[...] = times(asked[...].reshape(8 * SLOTS, N), tt).reshape(8, SLOTS, N)
    answers.start()
    tt_ref[...] = tt
    total = times(ask[8], tt)
    for part in (halo, first, asks):
        part.drain()
    answers.arrive()
    for n in range(8):
        total = total + answered[n]
    second.start(*observe(1, total, observed, precision, owned))
    gram_ref[...], proj_ref[...] = second.finish(mark.at[1], pick.at[1])
    for part in (answers, second):
        part.drain()


CHUNK = 1024


def last_kernel(gram, proj, tt_ref, ens, out, cells, moved, in_sem, out_sem):
    chunks = ROWS * COLS // CHUNK
    load = pltpu.make_async_copy(ens, cells, in_sem)
    load.start()
    tt = transform_t(gram[...], proj[...])
    both = jnp.dot(tt, tt_ref[...], precision=lax.Precision.HIGHEST, preferred_element_type=F32)
    high = both.astype(BF16)
    low = (both - high.astype(F32)).astype(BF16)
    right = jnp.concatenate(
        [jnp.concatenate([high, high], axis=1), jnp.concatenate([low, jnp.zeros_like(low)], axis=1)], axis=0
    )
    stores = []
    load.wait()
    for i in range(chunks):
        rows = pl.ds(i * CHUNK, CHUNK)
        xs = cells[rows, :]
        xh = xs.astype(BF16)
        xl = (xs - xh.astype(F32)).astype(BF16)
        res = lax.dot_general(
            jnp.concatenate([xh, xl], axis=1), right, (((1,), (1,)), ((), ())), preferred_element_type=F32
        )
        moved[rows, :] = res[:, :N] + res[:, N:]
        c = pltpu.make_async_copy(moved.at[rows], out.at[rows], out_sem.at[i])
        c.start()
        stores.append(c)
    for c in stores:
        c.wait()


def shape(*dims):
    return jax.ShapeDtypeStruct(dims, F32)


VM = pl.BlockSpec(memory_space=pltpu.VMEM)
HBM = pl.BlockSpec(memory_space=pltpu.HBM)


def local(ensemble, observed, precision, interp_weight, stencil, owned, pattern):
    cells = ensemble.reshape(ROWS, COLS, 1, N)
    small = (
        observed.reshape(2, 1, SLOTS),
        precision.reshape(2, 1, SLOTS),
        interp_weight.reshape(2, 4, SLOTS),
        stencil.reshape(2, 4, SLOTS),
        owned.reshape(2, 1, SLOTS),
        pattern.transpose(0, 1, 3, 2, 4).reshape(2, 5, 1, LONS),
    )
    gram, proj, tt = pl.pallas_call(
        main_kernel,
        out_shape=(shape(N, N), shape(1, N), shape(N, N)),
        in_specs=[HBM] * 7,
        out_specs=(VM, VM, VM),
        scratch_shapes=[pltpu.SMEM(a.shape, a.dtype) for a in small]
        + [
            pltpu.VMEM((ROWS + 2, COLS + 2, 1, N), F32),
            pltpu.VMEM((SLOTS, N), F32),
            pltpu.VMEM((9, SLOTS, N), F32),
            pltpu.VMEM((8, SLOTS, N), F32),
            pltpu.VMEM((8, SLOTS, N), F32),
            pltpu.VMEM((8, SLOTS, N), F32),
            pltpu.VMEM((5, LONS, PAIRS, 2, N), BF16),
            pltpu.VMEM((5, LONS, PAIRS, 2, N), BF16),
            pltpu.VMEM((2, 5, LONS, PAIRS, 2, N), BF16),
            pltpu.VMEM((5, LONS, PAIRS, 2, N), BF16),
            pltpu.VMEM((2, 5, 16, LONS * PAIRS * 2), BF16),
            pltpu.SemaphoreType.DMA((len(small),)),
            pltpu.SemaphoreType.DMA,
            pltpu.SemaphoreType.REGULAR,
            pltpu.SemaphoreType.DMA((8,)),
            pltpu.SemaphoreType.DMA((6,)),
            pltpu.SemaphoreType.DMA((6,)),
        ]
        + [pltpu.SemaphoreType.DMA((1 + len(GROUPS) + 2 * len(NEAR),))] * 2,
        compiler_params=pltpu.CompilerParams(collective_id=0, has_side_effects=True, vmem_limit_bytes=VMEM_BYTES),
        name="main",
    )(*(pltpu.with_memory_space_constraint(a, pltpu.HBM) for a in (cells,) + small))
    chunks = ROWS * COLS // CHUNK
    out = pl.pallas_call(
        last_kernel,
        out_shape=shape(ROWS * COLS, N),
        in_specs=[VM, VM, VM, HBM],
        out_specs=HBM,
        scratch_shapes=[
            pltpu.VMEM((ROWS * COLS, N), F32),
            pltpu.VMEM((ROWS * COLS, N), F32),
            pltpu.SemaphoreType.DMA,
            pltpu.SemaphoreType.DMA((chunks,)),
        ],
        compiler_params=pltpu.CompilerParams(vmem_limit_bytes=VMEM_BYTES),
        name="last",
    )(gram, proj, tt, pltpu.with_memory_space_constraint(ensemble.reshape(ROWS * COLS, N), pltpu.HBM))
    return out.reshape(ROWS, COLS, N)


def solution(mesh):
    placed = (
        P("lat", "lon", None),
        P(None, "lat", "lon", None),
        P(None, "lat", "lon", None),
        P(None, "lat", "lon", None, None),
        P(None, "lat", "lon", None, None),
        P(None, "lat", "lon", None),
        P(None, "lat", "lon", None, None),
    )
    return jax.shard_map(
        local, mesh=mesh, in_specs=placed, out_specs=P("lat", "lon", None), check_vma=False
    )
```
